768 devices in a mesh: row: 8 (over x, core), col: 96 (over z, y).
Axes of the slice: x: 4, y: 8, z: 12, core: 2. Of those that a mesh axis runs over, the one named last changes fastest.
Arguments:
- features: float32 [3, 8, 512, 768], P(None, 'row'), may hold values from -6 to 6
- ridge: float32 [3, 8, 512], P(None, 'row'), may hold values from 0.5 to 4
Outputs:
- schur: float32 [3, 8, 512, 1, 96, 128], P(None, 'row', None, None, 'col')
- panel: float32 [3, 8, 512, 512], P(None, 'row')
The draws below stay inside these ranges and needn't reach their ends.
All inputs are finite; a program needn't handle non-finite values.
Results may differ from the reference program's by a relative error of at most 0.00017.
Values sent between devices are 32-bit elements; how exact they have to be, the bound alone decides.
No kernel may reach another device: no remote copies, remote signals or barrier semaphores. Data moves between devices by JAX's collectives and lax.ppermute only.
A program may use at most 64 MiB of HBM per device.

```python
import math
import jax
import jax.numpy as jnp
from jax import lax

F = 768
B = 512
CB = 128
RT = 3
CT = 1
N_ROW = 8
N_COL = 96


def steps_of(stream_key, extent, shards, least, high):
    gain = 1.0
    for position, parts in shards:
        draws = jax.random.uniform(jax.random.fold_in(jax.random.fold_in(stream_key, 6), position), (parts,), jnp.float32, least / len(shards), high / len(shards))
        gain = gain * jnp.repeat(jnp.exp(draws), extent[position] // parts).reshape((-1,) + (1,) * (len(extent) - 1 - position))
    return gain


def normal_values(key, shape, deviation, most, shards=(), kind=jnp.bfloat16):
    loudness = steps_of(key, shape, shards, -0.22, 0.18) if shards else 1.0
    entries = jax.random.normal(key, shape, jnp.float32) * deviation * loudness
    return jnp.minimum(jnp.maximum(entries, -most), most).astype(kind)


def setup_inputs(seed: int = 0) -> dict:
    streams_of = jax.random.split(jax.random.key(seed), 3)
    features = normal_values(streams_of[0], (RT, N_ROW, B, F), 1.0, 6.0, ((1, 8),), jnp.float32)
    ridge = jnp.clip(jnp.exp(math.log(4.0) - 2.0794415 * jax.random.uniform(streams_of[1], (RT, N_ROW, B), jnp.float32) ** steps_of(streams_of[1], (RT, N_ROW, B), ((1, 8),), -0.2, 0.2)), 0.5, 4.0)
    return dict(features=features, ridge=ridge)


def kernel_of(left, right):
    inner = jnp.dot(left.astype(jnp.float32), right.T.astype(jnp.float32), precision=lax.Precision.HIGHEST, preferred_element_type=jnp.float32)
    return jnp.square(inner / F + 1.0)

def reference(features, ridge):
    samples = features.reshape(-1, F)
    ridge_all = ridge.reshape(-1)
    count = samples.shape[0]
    panel_feat = samples[:B]
    block = kernel_of(panel_feat, panel_feat) + jnp.diag(ridge_all[:B])
    lower = jnp.linalg.cholesky(block)
    match = jnp.arange(count, dtype=jnp.int32)[:, None] == jnp.arange(B, dtype=jnp.int32)[None, :]
    kp_block = kernel_of(samples, panel_feat) + jnp.where(match, ridge_all[:B][None, :], jnp.float32(0.0))
    panel = jax.scipy.linalg.solve_triangular(lower, kp_block.T, lower=True).T
    whole = kernel_of(samples, samples) + jnp.diag(ridge_all)
    schur = whole - jnp.dot(panel.astype(jnp.float32), panel.T.astype(jnp.float32), precision=lax.Precision.HIGHEST, preferred_element_type=jnp.float32)
    return (schur.reshape(RT, N_ROW, B, CT, N_COL, CB), panel.reshape(RT, N_ROW, B, B))
```

```python
import jax
import jax.numpy as jnp
from jax import lax
from jax.experimental import pallas as pl
from jax.experimental.pallas import tpu as pltpu
from jax.sharding import PartitionSpec as P

F32 = jnp.float32
BF16 = jnp.bfloat16
NB = 128
TN = (((1,), (1,)), ((), ()))


def split(a):
    hi = a.astype(BF16)
    return hi, (a - hi.astype(F32)).astype(BF16)


def dot3(a, b):
    one = lambda x, y: lax.dot_general(x, y, TN, preferred_element_type=F32)
    return one(a[0], b[0]) + (one(a[0], b[1]) + one(a[1], b[0]))


def dotf(a, b):
    return lax.dot_general(
        a, b, TN, precision=lax.Precision.HIGHEST, preferred_element_type=F32
    )


def lanes(v, k):
    return jnp.broadcast_to(v[:, k : k + 1], (8, NB))


def micro(upper, inv, t, cols_ref):
    row, low, o = upper[t], inv[t], 8 * t
    for k in range(8):
        cols_ref[8 * k : 8 * k + 8, :] = lanes(row, o + k)
    s = {}
    for k in range(8):
        for i in range(k, 8):
            s[i, k] = jnp.broadcast_to(cols_ref[8 * k + i : 8 * k + i + 1, :], (8, NB))
    v = [jnp.broadcast_to(row[i : i + 1, :], (8, NB)) for i in range(8)]
    w = [jnp.broadcast_to(low[i : i + 1, :], (8, NB)) for i in range(8)]
    u = {r: [lanes(upper[r], o + k) for k in range(8)] for r in range(t + 1, 16)}
    scale = []
    for k in range(8):
        rs = lax.rsqrt(s[k, k])
        scale.append(rs)
        v[k] = v[k] * rs
        w[k] = w[k] * rs
        for i in range(k + 1, 8):
            s[i, k] = s[i, k] * rs
        for j in range(k + 1, 8):
            for i in range(j, 8):
                s[i, j] = s[i, j] - s[i, k] * s[j, k]
        for i in range(k + 1, 8):
            v[i] = v[i] - s[i, k] * v[k]
            w[i] = w[i] - s[i, k] * w[k]
    upper, inv = list(upper), list(inv)
    if t < 15:
        r = t + 1
        for k in range(8):
            c = u[r][k]
            for m in range(k):
                c = c - u[r][m] * s[k, m]
            c = c * scale[k]
            u[r][k] = c
            upper[r] = upper[r] - c * v[k]
            inv[r] = inv[r] - c * w[k]
    if t < 14:
        vb, wb = list(v), list(w)
        for k in range(7, -1, -1):
            for m in range(k + 1, 8):
                vb[k] = vb[k] - s[m, k] * vb[m]
                wb[k] = wb[k] - s[m, k] * wb[m]
            vb[k] = vb[k] * scale[k]
            wb[k] = wb[k] * scale[k]
        for r in range(t + 2, 16):
            for k in range(8):
                upper[r] = upper[r] - u[r][k] * vb[k]
                inv[r] = inv[r] - u[r][k] * wb[k]
    sub = lax.broadcasted_iota(jnp.int32, (8, NB), 0)
    a, b = v[0], w[0]
    for k in range(1, 8):
        a = jnp.where(sub == k, v[k], a)
        b = jnp.where(sub == k, w[k], b)
    upper[t], inv[t] = a, b
    return upper, inv


def factor(block, cols_ref):
    upper = [block[8 * i : 8 * i + 8, :] for i in range(16)]
    sub = lax.broadcasted_iota(jnp.int32, (8, NB), 0)
    lane = lax.broadcasted_iota(jnp.int32, (8, NB), 1)
    inv = [jnp.where(lane == sub + 8 * i, F32(1.0), F32(0.0)) for i in range(16)]
    for t in range(16):
        upper, inv = micro(upper, inv, t, cols_ref.at[64 * (t % 2) : 64 * (t % 2) + 64])
    return upper, inv


def tile_of(inner, width):
    return jnp.square(inner / width + 1.0)


def match(shape, delta):
    rows = lax.broadcasted_iota(jnp.int32, shape, 0)
    cols = lax.broadcasted_iota(jnp.int32, shape, 1)
    return rows - cols == delta


def panel_kernel(
    where_ref, feat_ref, ridge_ref, a0_ref, b0_ref, a1_ref, b1_ref, col_ref, schur_ref, panel_ref,
    pan_hi, pan_lo, col_hi, col_lo, mat, low_hi, low_lo, inv_hi, inv_lo, pc_hi, pc_lo, cols_ref,
):
    tiles, width, feat = feat_ref.shape
    n_rowdev = 8
    nb = width // NB
    row_idx, col_idx = where_ref[0], where_ref[1]
    half = width // 2
    lines = []
    for h, (a, b) in enumerate(((a0_ref, b0_ref), (a1_ref, b1_ref))):
        pan_hi[h * half : (h + 1) * half, :], pan_lo[h * half : (h + 1) * half, :] = split(
            a[:half, :] + b[:half, :]
        )
        lines.append(a[half : half + 1, :half] + b[half : half + 1, :half])
    ridge = jnp.concatenate(lines, axis=1)
    col_hi[...], col_lo[...] = split(col_ref[...])
    for b in range(nb):
        lo = b * NB
        p = (pan_hi[lo : lo + NB, :], pan_lo[lo : lo + NB, :])
        block = tile_of(dot3((pan_hi[lo:, :], pan_lo[lo:, :]), p), feat)
        mat[lo:, lo : lo + NB] = block + jnp.where(
            match(block.shape, 0), ridge[:, lo : lo + NB], F32(0.0)
        )
    for b in range(nb):
        lo, hi = b * NB, (b + 1) * NB
        upper, inv = factor(mat[lo:hi, lo:hi], cols_ref)
        inv = jnp.concatenate(inv, axis=0)
        inv_hi[b], inv_lo[b] = split(inv)
        if b + 1 < nb:
            below = dotf(mat[hi:, lo:hi], inv)
            low_hi[hi:, lo:hi], low_lo[hi:, lo:hi] = split(below)
            for c in range(b + 1, nb):
                d = (c - b - 1) * NB
                mat[c * NB :, c * NB : (c + 1) * NB] -= dotf(below[d:, :], below[d : d + NB, :])

    def solve(samples, delta):
        done = []
        for b in range(nb):
            lo, hi = b * NB, (b + 1) * NB
            t = tile_of(dot3(samples, (pan_hi[lo:hi, :], pan_lo[lo:hi, :])), feat)
            t = t + jnp.where(match(t.shape, lo - delta), ridge[:, lo:hi], F32(0.0))
            for c in range(b):
                t = t - dot3(
                    done[c][0], (low_hi[lo:hi, c * NB : (c + 1) * NB], low_lo[lo:hi, c * NB : (c + 1) * NB])
                )
            x = dot3(split(t), (inv_hi[b], inv_lo[b]))
            done.append((split(x), x))
        return done

    big = jnp.int32(1 << 20)
    first = col_idx * NB
    diag = ridge_ref[
        first // (width * n_rowdev), :, pl.ds(pl.multiple_of(first % width, NB), NB)
    ]
    done = solve((col_hi[...], col_lo[...]), jnp.where(first < width, first, big))
    for b in range(nb):
        pc_hi[:, b * NB : (b + 1) * NB], pc_lo[:, b * NB : (b + 1) * NB] = done[b][0]

    step = 256
    per = width // step

    def body(i, carry):
        t, off = i // per, (i % per) * step
        x = split(feat_ref[t, pl.ds(off, step), :])
        own = (t * n_rowdev + row_idx) * width + off
        done = solve(x, jnp.where(own < width, own, big))
        g = tile_of(dot3(x, (col_hi[...], col_lo[...])), feat)
        g = g + jnp.where(match(g.shape, first - own), diag, F32(0.0))
        for b in range(nb):
            lo, hi = b * NB, (b + 1) * NB
            panel_ref[t, pl.ds(off, step), lo:hi] = done[b][1]
            g = g - dot3(done[b][0], (pc_hi[:, lo:hi], pc_lo[:, lo:hi]))
        schur_ref[t, pl.ds(off, step), :] = g
        return carry

    lax.fori_loop(0, tiles * per, body, 0)


def panel_step(where, feats, ridge, pan, cols):
    tiles, width, feat = feats.shape
    vm = pl.BlockSpec(memory_space=pltpu.VMEM)
    return pl.pallas_call(
        panel_kernel,
        out_shape=(
            jax.ShapeDtypeStruct((tiles, width, NB), F32),
            jax.ShapeDtypeStruct((tiles, width, width), F32),
        ),
        in_specs=[pl.BlockSpec(memory_space=pltpu.SMEM)] + [vm] * 7,
        out_specs=(vm, vm),
        scratch_shapes=[
            pltpu.VMEM((width, feat), BF16),
            pltpu.VMEM((width, feat), BF16),
            pltpu.VMEM((NB, feat), BF16),
            pltpu.VMEM((NB, feat), BF16),
            pltpu.VMEM((width, width), F32),
            pltpu.VMEM((width, width), BF16),
            pltpu.VMEM((width, width), BF16),
            pltpu.VMEM((width // NB, NB, NB), BF16),
            pltpu.VMEM((width // NB, NB, NB), BF16),
            pltpu.VMEM((NB, width), BF16),
            pltpu.VMEM((NB, width), BF16),
            pltpu.VMEM((NB, NB), F32),
        ],
        compiler_params=pltpu.CompilerParams(vmem_limit_bytes=48 << 20),
        name="panel_step",
    )(where, feats, ridge, *pan, cols)


def moved(block, pairs):
    n_row, n_col = lax.axis_size("row"), lax.axis_size("col")
    del n_row
    links = [(a * n_col + q, b * n_col + q) for a, b in pairs for q in range(n_col)]
    return lax.ppermute(block, ("row", "col"), links)


def column_links():
    links = []
    for chip in range(4):
        for core in range(2):
            for y in range(8):
                for z in range(12):
                    step = (z - chip + 1) % 4 - 1
                    near = (z - step) % 12
                    same = y // 4 == core
                    want = (chip + step) % 4 * 2 + (0 if same else 1)
                    links.append(
                        ((chip * 2 + core) * 96 + z * 8 + y, want * 96 + near * 8 + (y if same else 7 - y))
                    )
    return links


def per_device(features, ridge):
    tiles, _, width, feat = features.shape
    row_idx = lax.axis_index("row")
    col_idx = lax.axis_index("col")
    half = width // 2
    own = []
    for h in range(2):
        line = jnp.pad(ridge[0, :, h * half : (h + 1) * half], ((0, 7), (0, feat - half)))
        own.append(jnp.concatenate([features[0, 0, h * half : (h + 1) * half], line], axis=0))
    chip, core = row_idx // 2, row_idx % 2
    y, z = col_idx % 8, col_idx // 8
    step = (z - chip + 1) % 4 - 1
    near = (z - step) % 12
    want = near * 8 + jnp.where(y // 4 == core, y, 7 - y)
    zero = jnp.int32(0)
    piece = lax.dynamic_slice(
        features, (want // 32, zero, (want % 4) * NB, zero), (1, 1, NB, feat)
    ).reshape(NB, feat)
    f0 = moved(own[0], [(0, 2)])
    g1 = moved(own[1], [(0, 6)])
    f1 = moved(own[1], [(0, 2)])
    g0 = moved(own[0], [(0, 6)])
    cols = lax.ppermute(piece, ("row", "col"), column_links())
    h0 = moved(f0, [(2, 4)])
    h1 = moved(g1, [(6, 4)])
    holder = row_idx == 0
    a0 = jnp.where(holder, own[0], F32(0.0)) + f0 + g0 + h0
    a1 = jnp.where(holder, own[1], F32(0.0)) + f1 + g1 + h1
    a0, cols = lax.optimization_barrier((a0, cols))
    swap = [(0, 1), (2, 3), (4, 5), (6, 7)]
    b0 = moved(a0, swap)
    b1 = moved(a1, swap)
    where = jnp.stack([row_idx, col_idx]).astype(jnp.int32)
    schur, panel = panel_step(
        where, features.reshape(tiles, width, feat), ridge, (a0, b0, a1, b1), cols
    )
    return (
        schur.reshape(tiles, 1, width, 1, 1, NB),
        panel.reshape(tiles, 1, width, width),
    )


def solution(mesh):
    in_specs = (P(None, "row", None, None), P(None, "row", None))
    out_specs = (P(None, "row", None, None, "col", None), P(None, "row", None, None))
    return jax.shard_map(
        per_device, mesh=mesh, in_specs=in_specs, out_specs=out_specs, check_vma=False
    )
```

```python
import jax
import jax.numpy as jnp
from jax import lax
from jax.experimental import pallas as pl
from jax.experimental.pallas import tpu as pltpu
from jax.sharding import PartitionSpec as P

F32 = jnp.float32
BF16 = jnp.bfloat16
NB = 128
TN = (((1,), (1,)), ((), ()))


def split(a):
    hi = a.astype(BF16)
    return hi, (a - hi.astype(F32)).astype(BF16)


def dot3(a, b):
    one = lambda x, y: lax.dot_general(x, y, TN, preferred_element_type=F32)
    return one(a[0], b[0]) + (one(a[0], b[1]) + one(a[1], b[0]))


def dotf(a, b):
    return lax.dot_general(
        a, b, TN, precision=lax.Precision.HIGHEST, preferred_element_type=F32
    )


def lanes(v, k):
    return jnp.broadcast_to(v[:, k : k + 1], (8, NB))


def micro(upper, inv, t, cols_ref):
    row, low, o = upper[t], inv[t], 8 * t
    for k in range(8):
        cols_ref[8 * k : 8 * k + 8, :] = lanes(row, o + k)
    s = {}
    for k in range(8):
        for i in range(k, 8):
            s[i, k] = jnp.broadcast_to(cols_ref[8 * k + i : 8 * k + i + 1, :], (8, NB))
    v = [jnp.broadcast_to(row[i : i + 1, :], (8, NB)) for i in range(8)]
    w = [jnp.broadcast_to(low[i : i + 1, :], (8, NB)) for i in range(8)]
    u = {r: [lanes(upper[r], o + k) for k in range(8)] for r in range(t + 1, 16)}
    scale = []
    for k in range(8):
        rs = lax.rsqrt(s[k, k])
        scale.append(rs)
        v[k] = v[k] * rs
        w[k] = w[k] * rs
        for i in range(k + 1, 8):
            s[i, k] = s[i, k] * rs
        for j in range(k + 1, 8):
            for i in range(j, 8):
                s[i, j] = s[i, j] - s[i, k] * s[j, k]
        for i in range(k + 1, 8):
            v[i] = v[i] - s[i, k] * v[k]
            w[i] = w[i] - s[i, k] * w[k]
    upper, inv = list(upper), list(inv)
    if t < 15:
        r = t + 1
        for k in range(8):
            c = u[r][k]
            for m in range(k):
                c = c - u[r][m] * s[k, m]
            c = c * scale[k]
            u[r][k] = c
            upper[r] = upper[r] - c * v[k]
            inv[r] = inv[r] - c * w[k]
    if t < 14:
        vb, wb = list(v), list(w)
        for k in range(7, -1, -1):
            for m in range(k + 1, 8):
                vb[k] = vb[k] - s[m, k] * vb[m]
                wb[k] = wb[k] - s[m, k] * wb[m]
            vb[k] = vb[k] * scale[k]
            wb[k] = wb[k] * scale[k]
        for r in range(t + 2, 16):
            for k in range(8):
                upper[r] = upper[r] - u[r][k] * vb[k]
                inv[r] = inv[r] - u[r][k] * wb[k]
    sub = lax.broadcasted_iota(jnp.int32, (8, NB), 0)
    a, b = v[0], w[0]
    for k in range(1, 8):
        a = jnp.where(sub == k, v[k], a)
        b = jnp.where(sub == k, w[k], b)
    upper[t], inv[t] = a, b
    return upper, inv


def factor(block, cols_ref, work=()):
    upper = [block[8 * i : 8 * i + 8, :] for i in range(16)]
    sub = lax.broadcasted_iota(jnp.int32, (8, NB), 0)
    lane = lax.broadcasted_iota(jnp.int32, (8, NB), 1)
    inv = [jnp.where(lane == sub + 8 * i, F32(1.0), F32(0.0)) for i in range(16)]
    for t in range(16):
        for job in work[len(work) * t // 16 : len(work) * (t + 1) // 16]:
            job()
        upper, inv = micro(upper, inv, t, cols_ref.at[64 * (t % 2) : 64 * (t % 2) + 64])
    return upper, inv


def tile_of(inner, width):
    return jnp.square(inner / width + 1.0)


def match(shape, delta):
    rows = lax.broadcasted_iota(jnp.int32, shape, 0)
    cols = lax.broadcasted_iota(jnp.int32, shape, 1)
    return rows - cols == delta


def kernel_tile(left, right, delta, ridge, feat):
    block = tile_of(dot3(left, right), feat)
    return block + jnp.where(match(block.shape, delta), ridge, F32(0.0))


STEP = 192
FAR = 1 << 20


def first_kernel(
    where_ref, rows_hbm, a_ref, b_ref,
    panel_hbm, p_hi, p_lo, pan_hi, pan_lo, line_ref, inv_hi, inv_lo, low_hi, low_lo,
    rows, kp, out, cols_ref, in_sem, out_sem,
):
    count, feat = rows.shape
    half = kp.shape[1]
    load = pltpu.make_async_copy(rows_hbm, rows, in_sem)
    load.start()
    row_idx = where_ref[0]
    pan_hi[...], pan_lo[...] = split(a_ref[:half, :] + b_ref[:half, :])
    line = a_ref[half : half + 1, :half] + b_ref[half : half + 1, :half]
    line_ref[...] = jnp.broadcast_to(line, (8, half))
    pan = (pan_hi[...], pan_lo[...])
    k11 = kernel_tile(pan, (pan_hi[:NB, :], pan_lo[:NB, :]), 0, line[:, :NB], feat)
    k22 = kernel_tile(
        (pan_hi[NB:, :], pan_lo[NB:, :]), (pan_hi[NB:, :], pan_lo[NB:, :]), 0, line[:, NB:], feat
    )
    load.wait()

    def tiles(i):
        n = i * STEP
        x = split(rows[n : n + STEP, :])
        g = tile_of(dot3(x, (pan_hi[...], pan_lo[...])), feat)
        if n < 512:
            g = g + jnp.where(match(g.shape, jnp.where(row_idx == 0, -n, FAR)), line, F32(0.0))
        kp[n : n + STEP, :] = g

    _, inv = factor(k11[:NB], cols_ref, [lambda i=i: tiles(i) for i in range(count // STEP)])
    inv0 = jnp.concatenate(inv, axis=0)
    inv_hi[0], inv_lo[0] = split(inv0)
    l10 = dotf(k11[NB:], inv0)
    low_hi[...], low_lo[...] = split(l10)
    s11 = k22 - dotf(l10, l10)

    def solve(i):
        n = i * STEP
        x = dot3(split(kp[n : n + STEP, :NB]), (inv_hi[0], inv_lo[0]))
        out[n : n + STEP, :NB] = x
        hi, lo = split(x)
        p_hi[n : n + STEP, :NB], p_lo[n : n + STEP, :NB] = hi, lo
        kp[n : n + STEP, NB:] = kp[n : n + STEP, NB:] - dot3((hi, lo), (low_hi[...], low_lo[...]))

    _, inv = factor(s11, cols_ref, [lambda i=i: solve(i) for i in range(count // STEP)])
    inv_hi[1], inv_lo[1] = split(jnp.concatenate(inv, axis=0))
    x = dot3(split(kp[:, NB:]), (inv_hi[1], inv_lo[1]))
    out[:, NB:] = x
    p_hi[:, NB:], p_lo[:, NB:] = split(x)
    store = pltpu.make_async_copy(out, panel_hbm.at[:, pl.ds(0, half)], out_sem)
    store.start()
    store.wait()


def second_kernel(
    where_ref, rows_hbm, a_ref, b_ref, ca_ref, cb_ref, ridge_ref, old_panel,
    p_hi, p_lo, pan_hi, pan_lo, line_ref, inv_hi, inv_lo, low_hi, low_lo,
    schur_ref, panel_hbm,
    rows, kp, out, q_hi, q_lo, l2_hi, l2_lo, l32_hi, l32_lo, nv_hi, nv_lo, col_hi, col_lo, kc, pc_hi, pc_lo,
    cols_ref, in_sem, out_sem,
):
    count, feat = rows.shape
    half = kp.shape[1]
    load = pltpu.make_async_copy(rows_hbm, rows, in_sem)
    load.start()
    row_idx, col_idx = where_ref[0], where_ref[1]
    q_hi[...], q_lo[...] = split(a_ref[:half, :] + b_ref[:half, :])
    line = a_ref[half : half + 1, :half] + b_ref[half : half + 1, :half]
    col_hi[...], col_lo[...] = split(ca_ref[...] + cb_ref[...])
    new = (q_hi[...], q_lo[...])

    def lead(k, dst_hi, dst_lo):
        n0 = dot3(split(k[:, :NB]), (inv_hi[0], inv_lo[0]))
        s0 = split(n0)
        n1 = dot3(split(k[:, NB:] - dot3(s0, (low_hi[...], low_lo[...]))), (inv_hi[1], inv_lo[1]))
        s1 = split(n1)
        dst_hi[:, :NB], dst_lo[:, :NB] = s0
        dst_hi[:, NB:half], dst_lo[:, NB:half] = s1

    lead(tile_of(dot3(new, (pan_hi[...], pan_lo[...])), feat), l2_hi, l2_lo)
    k2 = kernel_tile(new, new, 0, line, feat) - dot3((l2_hi[...], l2_lo[...]), (l2_hi[...], l2_lo[...]))
    load.wait()

    def tiles(i):
        n = i * STEP
        x = split(rows[n : n + STEP, :])
        g = tile_of(dot3(x, (q_hi[...], q_lo[...])), feat)
        if half - n > -STEP and n < 512:
            g = g + jnp.where(match(g.shape, jnp.where(row_idx == 0, half - n, FAR)), line, F32(0.0))
        kp[n : n + STEP, :] = g - dot3(
            (p_hi[n : n + STEP, :], p_lo[n : n + STEP, :]), (l2_hi[...], l2_lo[...])
        )

    _, inv = factor(k2[:NB, :NB], cols_ref, [lambda i=i: tiles(i) for i in range(count // STEP)])
    inv2 = jnp.concatenate(inv, axis=0)
    nv_hi[0], nv_lo[0] = split(inv2)
    l32 = dotf(k2[NB:, :NB], inv2)
    l32_hi[...], l32_lo[...] = split(l32)
    s33 = k2[NB:, NB:] - dotf(l32, l32)
    first = col_idx * NB
    owner, n_tile = (col_idx // 4) % 8, col_idx // 32
    inner = (col_idx % 4) * NB
    diag = ridge_ref[n_tile, :, pl.ds(pl.multiple_of(inner, NB), NB)]
    corner = jnp.where(row_idx == owner, n_tile * 512 + inner, FAR)

    def columns():
        col = (col_hi[...], col_lo[...])
        lead(
            kernel_tile(col, (pan_hi[...], pan_lo[...]), -first, line_ref[:1, :], feat),
            pc_hi, pc_lo,
        )
        kc[...] = kernel_tile(col, new, half - first, line, feat) - dot3(
            (pc_hi[:, :half], pc_lo[:, :half]), (l2_hi[...], l2_lo[...])
        )
        x = split(dot3(split(kc[:, :NB]), (nv_hi[0], nv_lo[0])))
        pc_hi[:, half : half + NB], pc_lo[:, half : half + NB] = x
        kc[:, NB:] = kc[:, NB:] - dot3(x, (l32_hi[...], l32_lo[...]))

    def solve(i):
        n = i * STEP
        x = dot3(split(kp[n : n + STEP, :NB]), (nv_hi[0], nv_lo[0]))
        out[n : n + STEP, :NB] = x
        s = split(x)
        kp[n : n + STEP, NB:] = kp[n : n + STEP, NB:] - dot3(s, (l32_hi[...], l32_lo[...]))
        g = tile_of(dot3(split(rows[n : n + STEP, :]), (col_hi[...], col_lo[...])), feat)
        g = g + jnp.where(match(g.shape, corner - n), diag, F32(0.0))
        g = g - dot3(
            (p_hi[n : n + STEP, :], p_lo[n : n + STEP, :]), (pc_hi[:, :half], pc_lo[:, :half])
        )
        schur_ref[n : n + STEP, :] = g - dot3(
            s, (pc_hi[:, half : half + NB], pc_lo[:, half : half + NB])
        )

    _, inv = factor(
        s33, cols_ref, [columns] + [lambda i=i: solve(i) for i in range(count // STEP)]
    )
    nv_hi[1], nv_lo[1] = split(jnp.concatenate(inv, axis=0))
    pc = split(dot3(split(kc[:, NB:]), (nv_hi[1], nv_lo[1])))
    x = dot3(split(kp[:, NB:]), (nv_hi[1], nv_lo[1]))
    out[:, NB:] = x
    store = pltpu.make_async_copy(out, panel_hbm.at[:, pl.ds(half, half)], out_sem)
    store.start()
    schur_ref[...] = schur_ref[...] - dot3(split(x), pc)
    store.wait()


VM = pl.BlockSpec(memory_space=pltpu.VMEM)
SM = pl.BlockSpec(memory_space=pltpu.SMEM)
HB = pl.BlockSpec(memory_space=pltpu.HBM)


def shaped(*shape, kind=F32):
    return jax.ShapeDtypeStruct(shape, kind)


def first_step(where, rows, pair):
    count, feat = rows.shape
    half = 256
    return pl.pallas_call(
        first_kernel,
        out_shape=(
            shaped(count, 2 * half),
            shaped(count, half, kind=BF16),
            shaped(count, half, kind=BF16),
            shaped(half, feat, kind=BF16),
            shaped(half, feat, kind=BF16),
            shaped(8, half),
            shaped(2, NB, NB, kind=BF16),
            shaped(2, NB, NB, kind=BF16),
            shaped(NB, NB, kind=BF16),
            shaped(NB, NB, kind=BF16),
        ),
        in_specs=[SM, HB, VM, VM],
        out_specs=(HB,) + (VM,) * 9,
        scratch_shapes=[
            pltpu.VMEM((count, feat), F32),
            pltpu.VMEM((count, half), F32),
            pltpu.VMEM((count, half), F32),
            pltpu.VMEM((NB, NB), F32),
            pltpu.SemaphoreType.DMA,
            pltpu.SemaphoreType.DMA,
        ],
        compiler_params=pltpu.CompilerParams(vmem_limit_bytes=20 << 20),
        cost_estimate=pl.CostEstimate(flops=5 * 10**9, bytes_accessed=40 * 10**6, transcendentals=0),
        name="first_step",
    )(where, rows, *pair)


def second_step(where, rows, pair, cols, ridge, kept):
    count, feat = rows.shape
    half = 256
    return pl.pallas_call(
        second_kernel,
        out_shape=(shaped(count, NB), shaped(count, 2 * half)),
        in_specs=[SM, HB] + [VM] * 5 + [HB] + [VM] * 9,
        out_specs=(VM, HB),
        input_output_aliases={7: 1},
        scratch_shapes=[
            pltpu.VMEM((count, feat), F32),
            pltpu.VMEM((count, half), F32),
            pltpu.VMEM((count, half), F32),
            pltpu.VMEM((half, feat), BF16),
            pltpu.VMEM((half, feat), BF16),
            pltpu.VMEM((half, half), BF16),
            pltpu.VMEM((half, half), BF16),
            pltpu.VMEM((NB, NB), BF16),
            pltpu.VMEM((NB, NB), BF16),
            pltpu.VMEM((2, NB, NB), BF16),
            pltpu.VMEM((2, NB, NB), BF16),
            pltpu.VMEM((NB, feat), BF16),
            pltpu.VMEM((NB, feat), BF16),
            pltpu.VMEM((NB, half), F32),
            pltpu.VMEM((NB, half + NB), BF16),
            pltpu.VMEM((NB, half + NB), BF16),
            pltpu.VMEM((NB, NB), F32),
            pltpu.SemaphoreType.DMA,
            pltpu.SemaphoreType.DMA,
        ],
        compiler_params=pltpu.CompilerParams(vmem_limit_bytes=20 << 20),
        cost_estimate=pl.CostEstimate(flops=5 * 10**9, bytes_accessed=40 * 10**6, transcendentals=0),
        name="second_step",
    )(where, rows, *pair, *cols, ridge, *kept)


def prepare_kernel(where_ref, feats_ref, ridge_ref, own0, own1, piece, sems):
    half = own0.shape[0] - 8
    loads = [
        pltpu.make_async_copy(feats_ref.at[0, pl.ds(0, half)], own0.at[pl.ds(0, half)], sems.at[0]),
        pltpu.make_async_copy(feats_ref.at[0, pl.ds(half, half)], own1.at[pl.ds(0, half)], sems.at[1]),
        pltpu.make_async_copy(
            feats_ref.at[where_ref[1] // 32, pl.ds(pl.multiple_of(where_ref[1] % 4 * NB, NB), NB)],
            piece,
            sems.at[2],
        ),
    ]
    for load in loads:
        load.start()
    for h, own in enumerate((own0, own1)):
        own[half:, :half] = jnp.broadcast_to(ridge_ref[0, :, h * half : (h + 1) * half], (8, half))
        own[half:, half:] = jnp.zeros((8, own.shape[1] - half), F32)
    for load in loads:
        load.wait()


def prepare(where, feats, ridge):
    half, feat = 256, feats.shape[2]
    return pl.pallas_call(
        prepare_kernel,
        out_shape=(shaped(half + 8, feat), shaped(half + 8, feat), shaped(NB, feat)),
        in_specs=[SM, HB, VM],
        out_specs=(VM, VM, VM),
        scratch_shapes=[pltpu.SemaphoreType.DMA((3,))],
        name="prepare",
    )(where, feats, ridge)


def moved(block, hop):
    links = []
    for device in range(768):
        x, c, z, y = device // 192, device // 96 % 2, device % 96 // 8, device % 8
        to = hop(x, c, y, z)
        if to is not None:
            links.append((device, (to[0] % 4 * 2 + to[1]) * 96 + z * 8 + y))
    return lax.ppermute(block, ("row", "col"), links)


def along(start, stop):
    return lambda x, c, y, z: (stop, 0) if (x, c) == (start, 0) else None


def fanned(step):
    return lambda x, c, y, z: (x + step, c) if (x, c) == (z % 4, y // 4) else None


def per_device(features, ridge):
    tiles, _, width, feat = features.shape
    row_idx = lax.axis_index("row")
    col_idx = lax.axis_index("col")
    where = jnp.stack([row_idx, col_idx]).astype(jnp.int32)
    feats = features.reshape(tiles, width, feat)
    own0, own1, piece = prepare(where, feats, ridge)
    g0 = moved(own0, along(0, 3))
    f0 = moved(own0, along(0, 1))
    d0 = moved(own0, along(0, 2))
    g1 = moved(own1, along(0, 3))
    f1 = moved(own1, along(0, 1))
    c1 = moved(piece, fanned(1))
    c2 = moved(piece, fanned(3))
    c3 = moved(piece, fanned(2))
    a0 = jnp.where(row_idx == 0, own0, F32(0.0)) + f0 + g0 + d0
    b0 = moved(a0, lambda x, c, y, z: (x, 1) if c == 0 else None)
    h1 = moved(g1, along(3, 2))
    rows = pltpu.with_memory_space_constraint(feats.reshape(tiles * width, feat), pltpu.HBM)
    kept = first_step(where, rows, (a0, b0))
    a1 = jnp.where(row_idx == 0, own1, F32(0.0)) + f1 + g1 + h1
    b1 = moved(a1, lambda x, c, y, z: (x, 1) if c == 0 else None)
    holder = row_idx == col_idx // 4 % 8
    ca = jnp.where(holder, piece, F32(0.0)) + c1 + c2 + c3
    cb = moved(ca, lambda x, c, y, z: (x, 1 - c) if c == y // 4 else None)
    schur, panel = second_step(where, rows, (a1, b1), (ca, cb), ridge, kept)
    return (
        schur.reshape(tiles, 1, width, 1, 1, NB),
        panel.reshape(tiles, 1, width, width),
    )


def solution(mesh):
    in_specs = (P(None, "row", None, None), P(None, "row", None))
    out_specs = (P(None, "row", None, None, "col", None), P(None, "row", None, None))
    return jax.shard_map(
        per_device, mesh=mesh, in_specs=in_specs, out_specs=out_specs, check_vma=False
    )
```

```python
import jax
import jax.numpy as jnp
from jax import lax
from jax.experimental import pallas as pl
from jax.experimental.pallas import tpu as pltpu
from jax.sharding import PartitionSpec as P

F32 = jnp.float32
BF16 = jnp.bfloat16
NB = 128
TN = (((1,), (1,)), ((), ()))


def split(a):
    hi = a.astype(BF16)
    return hi, (a - hi.astype(F32)).astype(BF16)


def dot3(a, b):
    one = lambda x, y: lax.dot_general(x, y, TN, preferred_element_type=F32)
    return one(a[0], b[0]) + (one(a[0], b[1]) + one(a[1], b[0]))


def dotf(a, b):
    return lax.dot_general(
        a, b, TN, precision=lax.Precision.HIGHEST, preferred_element_type=F32
    )


def lanes(v, k):
    return jnp.broadcast_to(v[:, k : k + 1], (8, NB))


def micro(upper, inv, t, cols_ref):
    row, low, o = upper[t], inv[t], 8 * t
    for k in range(8):
        cols_ref[8 * k : 8 * k + 8, :] = lanes(row, o + k)
    s = {}
    for k in range(8):
        for i in range(k, 8):
            s[i, k] = jnp.broadcast_to(cols_ref[8 * k + i : 8 * k + i + 1, :], (8, NB))
    v = [jnp.broadcast_to(row[i : i + 1, :], (8, NB)) for i in range(8)]
    w = [jnp.broadcast_to(low[i : i + 1, :], (8, NB)) for i in range(8)]
    u = {r: [lanes(upper[r], o + k) for k in range(8)] for r in range(t + 1, 16)}
    scale = []
    for k in range(8):
        rs = lax.rsqrt(s[k, k])
        scale.append(rs)
        v[k] = v[k] * rs
        w[k] = w[k] * rs
        for i in range(k + 1, 8):
            s[i, k] = s[i, k] * rs
        for j in range(k + 1, 8):
            for i in range(j, 8):
                s[i, j] = s[i, j] - s[i, k] * s[j, k]
        for i in range(k + 1, 8):
            v[i] = v[i] - s[i, k] * v[k]
            w[i] = w[i] - s[i, k] * w[k]
    upper, inv = list(upper), list(inv)
    if t < 15:
        r = t + 1
        for k in range(8):
            c = u[r][k]
            for m in range(k):
                c = c - u[r][m] * s[k, m]
            c = c * scale[k]
            u[r][k] = c
            upper[r] = upper[r] - c * v[k]
            inv[r] = inv[r] - c * w[k]
    if t < 14:
        vb, wb = list(v), list(w)
        for k in range(7, -1, -1):
            for m in range(k + 1, 8):
                vb[k] = vb[k] - s[m, k] * vb[m]
                wb[k] = wb[k] - s[m, k] * wb[m]
            vb[k] = vb[k] * scale[k]
            wb[k] = wb[k] * scale[k]
        for r in range(t + 2, 16):
            for k in range(8):
                upper[r] = upper[r] - u[r][k] * vb[k]
                inv[r] = inv[r] - u[r][k] * wb[k]
    sub = lax.broadcasted_iota(jnp.int32, (8, NB), 0)
    a, b = v[0], w[0]
    for k in range(1, 8):
        a = jnp.where(sub == k, v[k], a)
        b = jnp.where(sub == k, w[k], b)
    upper[t], inv[t] = a, b
    return upper, inv


def factor(block, cols_ref, work=()):
    upper = [block[8 * i : 8 * i + 8, :] for i in range(16)]
    sub = lax.broadcasted_iota(jnp.int32, (8, NB), 0)
    lane = lax.broadcasted_iota(jnp.int32, (8, NB), 1)
    inv = [jnp.where(lane == sub + 8 * i, F32(1.0), F32(0.0)) for i in range(16)]
    for t in range(16):
        for job in work[len(work) * t // 16 : len(work) * (t + 1) // 16]:
            job()
        upper, inv = micro(upper, inv, t, cols_ref.at[64 * (t % 2) : 64 * (t % 2) + 64])
    return upper, inv


def tile_of(inner, width):
    return jnp.square(inner / width + 1.0)


def match(shape, delta):
    rows = lax.broadcasted_iota(jnp.int32, shape, 0)
    cols = lax.broadcasted_iota(jnp.int32, shape, 1)
    return rows - cols == delta


def kernel_tile(left, right, delta, ridge, feat):
    block = tile_of(dot3(left, right), feat)
    return block + jnp.where(match(block.shape, delta), ridge, F32(0.0))


STEP = 192
FAR = 1 << 20


def first_kernel(
    where_ref, rows_hbm, a_ref, b_ref,
    panel_hbm, p_hi, p_lo, pan_hi_hbm, pan_lo_hbm, line_ref, inv_hi, inv_lo, low_hi, low_lo,
    rows, kp, out, pan_hi, pan_lo, cols_ref, in_sem, out_sems,
):
    count, feat = rows.shape
    half = kp.shape[1]
    load = pltpu.make_async_copy(rows_hbm, rows, in_sem)
    load.start()
    row_idx = where_ref[0]
    pan_hi[...], pan_lo[...] = split(a_ref[:half, :] + b_ref[:half, :])
    line = a_ref[half : half + 1, :half] + b_ref[half : half + 1, :half]
    line_ref[...] = jnp.broadcast_to(line, (8, half))
    stores = [
        pltpu.make_async_copy(pan_hi, pan_hi_hbm, out_sems.at[0]),
        pltpu.make_async_copy(pan_lo, pan_lo_hbm, out_sems.at[1]),
        pltpu.make_async_copy(out.at[0], panel_hbm.at[:, pl.ds(0, NB)], out_sems.at[2]),
        pltpu.make_async_copy(out.at[1], panel_hbm.at[:, pl.ds(NB, NB)], out_sems.at[3]),
    ]
    stores[0].start()
    stores[1].start()
    pan = (pan_hi[...], pan_lo[...])
    k11 = kernel_tile(pan, (pan_hi[:NB, :], pan_lo[:NB, :]), 0, line[:, :NB], feat)
    k22 = kernel_tile(
        (pan_hi[NB:, :], pan_lo[NB:, :]), (pan_hi[NB:, :], pan_lo[NB:, :]), 0, line[:, NB:], feat
    )
    load.wait()

    def tiles(i):
        n = i * STEP
        x = split(rows[n : n + STEP, :])
        g = tile_of(dot3(x, (pan_hi[...], pan_lo[...])), feat)
        if n < 512:
            g = g + jnp.where(match(g.shape, jnp.where(row_idx == 0, -n, FAR)), line, F32(0.0))
        kp[n : n + STEP, :] = g

    _, inv = factor(k11[:NB], cols_ref, [lambda i=i: tiles(i) for i in range(count // STEP)])
    inv0 = jnp.concatenate(inv, axis=0)
    inv_hi[0], inv_lo[0] = split(inv0)
    l10 = dotf(k11[NB:], inv0)
    low_hi[...], low_lo[...] = split(l10)
    s11 = k22 - dotf(l10, l10)

    def solve(i):
        n = i * STEP
        x = dot3(split(kp[n : n + STEP, :NB]), (inv_hi[0], inv_lo[0]))
        out[0, n : n + STEP, :] = x
        hi, lo = split(x)
        p_hi[n : n + STEP, :NB], p_lo[n : n + STEP, :NB] = hi, lo
        kp[n : n + STEP, NB:] = kp[n : n + STEP, NB:] - dot3((hi, lo), (low_hi[...], low_lo[...]))

    _, inv = factor(s11, cols_ref, [lambda i=i: solve(i) for i in range(count // STEP)])
    stores[2].start()
    inv_hi[1], inv_lo[1] = split(jnp.concatenate(inv, axis=0))
    x = dot3(split(kp[:, NB:]), (inv_hi[1], inv_lo[1]))
    out[1] = x
    stores[3].start()
    p_hi[:, NB:], p_lo[:, NB:] = split(x)
    for store in stores:
        store.wait()


def second_kernel(
    where_ref, rows_hbm, a_ref, b_ref, ridge_ref, old_panel,
    p_hi, p_lo, pan_hi_hbm, pan_lo_hbm, line_ref, inv_hi, inv_lo, low_hi, low_lo,
    schur_ref, panel_hbm,
    rows, kp, out, q_hi, q_lo, l2_hi, l2_lo, l32_hi, l32_lo, nv_hi, nv_lo, col_hi, col_lo, kc, pc_hi, pc_lo,
    pan_hi, pan_lo, cols_ref, in_sems, out_sems,
):
    count, feat = rows.shape
    half = kp.shape[1]
    early = [
        pltpu.make_async_copy(pan_hi_hbm, pan_hi, in_sems.at[0]),
        pltpu.make_async_copy(pan_lo_hbm, pan_lo, in_sems.at[1]),
    ]
    load = pltpu.make_async_copy(rows_hbm, rows, in_sems.at[2])
    for copy in early + [load]:
        copy.start()
    row_idx, col_idx = where_ref[0], where_ref[1]
    q_hi[...], q_lo[...] = split(a_ref[:half, :] + b_ref[:half, :])
    line = a_ref[half : half + 1, :half] + b_ref[half : half + 1, :half]
    tail = half + 8
    col_hi[...], col_lo[...] = split(a_ref[tail:, :] + b_ref[tail:, :])
    new = (q_hi[...], q_lo[...])

    def lead(k, dst_hi, dst_lo):
        n0 = dot3(split(k[:, :NB]), (inv_hi[0], inv_lo[0]))
        s0 = split(n0)
        n1 = dot3(split(k[:, NB:] - dot3(s0, (low_hi[...], low_lo[...]))), (inv_hi[1], inv_lo[1]))
        s1 = split(n1)
        dst_hi[:, :NB], dst_lo[:, :NB] = s0
        dst_hi[:, NB:half], dst_lo[:, NB:half] = s1

    k2 = kernel_tile(new, new, 0, line, feat)
    for copy in early:
        copy.wait()
    lead(tile_of(dot3(new, (pan_hi[...], pan_lo[...])), feat), l2_hi, l2_lo)
    k2 = k2 - dot3((l2_hi[...], l2_lo[...]), (l2_hi[...], l2_lo[...]))
    load.wait()

    def tiles(i):
        n = i * STEP
        x = split(rows[n : n + STEP, :])
        g = tile_of(dot3(x, (q_hi[...], q_lo[...])), feat)
        if half - n > -STEP and n < 512:
            g = g + jnp.where(match(g.shape, jnp.where(row_idx == 0, half - n, FAR)), line, F32(0.0))
        kp[n : n + STEP, :] = g - dot3(
            (p_hi[n : n + STEP, :], p_lo[n : n + STEP, :]), (l2_hi[...], l2_lo[...])
        )

    _, inv = factor(k2[:NB, :NB], cols_ref, [lambda i=i: tiles(i) for i in range(count // STEP)])
    inv2 = jnp.concatenate(inv, axis=0)
    nv_hi[0], nv_lo[0] = split(inv2)
    l32 = dotf(k2[NB:, :NB], inv2)
    l32_hi[...], l32_lo[...] = split(l32)
    s33 = k2[NB:, NB:] - dotf(l32, l32)
    first = col_idx * NB
    owner, n_tile = (col_idx // 4) % 8, col_idx // 32
    inner = (col_idx % 4) * NB
    diag = ridge_ref[n_tile, :, pl.ds(pl.multiple_of(inner, NB), NB)]
    corner = jnp.where(row_idx == owner, n_tile * 512 + inner, FAR)

    def columns():
        col = (col_hi[...], col_lo[...])
        lead(
            kernel_tile(col, (pan_hi[...], pan_lo[...]), -first, line_ref[:1, :], feat),
            pc_hi, pc_lo,
        )
        kc[...] = kernel_tile(col, new, half - first, line, feat) - dot3(
            (pc_hi[:, :half], pc_lo[:, :half]), (l2_hi[...], l2_lo[...])
        )
        x = split(dot3(split(kc[:, :NB]), (nv_hi[0], nv_lo[0])))
        pc_hi[:, half : half + NB], pc_lo[:, half : half + NB] = x
        kc[:, NB:] = kc[:, NB:] - dot3(x, (l32_hi[...], l32_lo[...]))

    def solve(i):
        n = i * STEP
        x = dot3(split(kp[n : n + STEP, :NB]), (nv_hi[0], nv_lo[0]))
        out[0, n : n + STEP, :] = x
        s = split(x)
        kp[n : n + STEP, NB:] = kp[n : n + STEP, NB:] - dot3(s, (l32_hi[...], l32_lo[...]))
        g = tile_of(dot3(split(rows[n : n + STEP, :]), (col_hi[...], col_lo[...])), feat)
        g = g + jnp.where(match(g.shape, corner - n), diag, F32(0.0))
        g = g - dot3(
            (p_hi[n : n + STEP, :], p_lo[n : n + STEP, :]), (pc_hi[:, :half], pc_lo[:, :half])
        )
        schur_ref[n : n + STEP, :] = g - dot3(
            s, (pc_hi[:, half : half + NB], pc_lo[:, half : half + NB])
        )

    _, inv = factor(
        s33, cols_ref, [columns] + [lambda i=i: solve(i) for i in range(count // STEP)]
    )
    stores = [
        pltpu.make_async_copy(
            out.at[i], panel_hbm.at[:, pl.ds(half + i * NB, NB)], out_sems.at[i]
        )
        for i in range(2)
    ]
    stores[0].start()
    nv_hi[1], nv_lo[1] = split(jnp.concatenate(inv, axis=0))
    pc = split(dot3(split(kc[:, NB:]), (nv_hi[1], nv_lo[1])))
    x = dot3(split(kp[:, NB:]), (nv_hi[1], nv_lo[1]))
    out[1] = x
    stores[1].start()
    schur_ref[...] = schur_ref[...] - dot3(split(x), pc)
    for store in stores:
        store.wait()


VM = pl.BlockSpec(memory_space=pltpu.VMEM)
SM = pl.BlockSpec(memory_space=pltpu.SMEM)
HB = pl.BlockSpec(memory_space=pltpu.HBM)


def shaped(*shape, kind=F32):
    return jax.ShapeDtypeStruct(shape, kind)


def first_step(where, rows, pair):
    count, feat = rows.shape
    half = 256
    return pl.pallas_call(
        first_kernel,
        out_shape=(
            shaped(count, 2 * half),
            shaped(count, half, kind=BF16),
            shaped(count, half, kind=BF16),
            shaped(half, feat, kind=BF16),
            shaped(half, feat, kind=BF16),
            shaped(8, half),
            shaped(2, NB, NB, kind=BF16),
            shaped(2, NB, NB, kind=BF16),
            shaped(NB, NB, kind=BF16),
            shaped(NB, NB, kind=BF16),
        ),
        in_specs=[SM, HB, VM, VM],
        out_specs=(HB, VM, VM, HB, HB) + (VM,) * 5,
        scratch_shapes=[
            pltpu.VMEM((count, feat), F32),
            pltpu.VMEM((count, half), F32),
            pltpu.VMEM((2, count, NB), F32),
            pltpu.VMEM((half, feat), BF16),
            pltpu.VMEM((half, feat), BF16),
            pltpu.VMEM((NB, NB), F32),
            pltpu.SemaphoreType.DMA,
            pltpu.SemaphoreType.DMA((4,)),
        ],
        compiler_params=pltpu.CompilerParams(vmem_limit_bytes=20 << 20),
        cost_estimate=pl.CostEstimate(flops=5 * 10**9, bytes_accessed=40 * 10**6, transcendentals=0),
        name="first_step",
    )(where, rows, *pair)


def second_step(where, rows, pair, ridge, kept):
    count, feat = rows.shape
    half = 256
    return pl.pallas_call(
        second_kernel,
        out_shape=(shaped(count, NB), shaped(count, 2 * half)),
        in_specs=[SM, HB] + [VM] * 3 + [HB, VM, VM, HB, HB] + [VM] * 5,
        out_specs=(VM, HB),
        input_output_aliases={5: 1},
        scratch_shapes=[
            pltpu.VMEM((count, feat), F32),
            pltpu.VMEM((count, half), F32),
            pltpu.VMEM((2, count, NB), F32),
            pltpu.VMEM((half, feat), BF16),
            pltpu.VMEM((half, feat), BF16),
            pltpu.VMEM((half, half), BF16),
            pltpu.VMEM((half, half), BF16),
            pltpu.VMEM((NB, NB), BF16),
            pltpu.VMEM((NB, NB), BF16),
            pltpu.VMEM((2, NB, NB), BF16),
            pltpu.VMEM((2, NB, NB), BF16),
            pltpu.VMEM((NB, feat), BF16),
            pltpu.VMEM((NB, feat), BF16),
            pltpu.VMEM((NB, half), F32),
            pltpu.VMEM((NB, half + NB), BF16),
            pltpu.VMEM((NB, half + NB), BF16),
            pltpu.VMEM((half, feat), BF16),
            pltpu.VMEM((half, feat), BF16),
            pltpu.VMEM((NB, NB), F32),
            pltpu.SemaphoreType.DMA((3,)),
            pltpu.SemaphoreType.DMA((2,)),
        ],
        compiler_params=pltpu.CompilerParams(vmem_limit_bytes=20 << 20),
        cost_estimate=pl.CostEstimate(flops=5 * 10**9, bytes_accessed=40 * 10**6, transcendentals=0),
        name="second_step",
    )(where, rows, *pair, ridge, *kept)


def prepare_kernel(where_ref, feats_ref, ridge_ref, own0, own1, piece, buf, sems):
    half = own0.shape[0] - 8
    full = half + 8
    starts = (0, full, 2 * full)
    loads = [
        pltpu.make_async_copy(feats_ref.at[0, pl.ds(0, half)], buf.at[pl.ds(0, half)], sems.at[0]),
        pltpu.make_async_copy(
            feats_ref.at[0, pl.ds(half, half)], buf.at[pl.ds(full, half)], sems.at[1]
        ),
        pltpu.make_async_copy(
            feats_ref.at[where_ref[2] // 32, pl.ds(pl.multiple_of(where_ref[2] % 4 * NB, NB), NB)],
            buf.at[pl.ds(2 * full, NB)],
            sems.at[2],
        ),
    ]
    stores = [
        pltpu.make_async_copy(buf.at[pl.ds(s, ref.shape[0])], ref, sems.at[3 + i])
        for i, (s, ref) in enumerate(zip(starts, (own0, own1, piece)))
    ]
    for load in loads:
        load.start()
    for h in range(2):
        low = starts[h] + half
        line = ridge_ref[0, :, h * half : (h + 1) * half]
        buf[low : low + 8, :half] = jnp.broadcast_to(line, (8, half))
        buf[low : low + 8, half:] = jnp.zeros((8, buf.shape[1] - half), F32)
    for load, store in zip(loads, stores):
        load.wait()
        store.start()
    for store in stores:
        store.wait()


def prepare(where, feats, ridge):
    half, feat = 256, feats.shape[2]
    return pl.pallas_call(
        prepare_kernel,
        out_shape=(shaped(half + 8, feat), shaped(half + 8, feat), shaped(NB, feat)),
        in_specs=[SM, HB, VM],
        out_specs=(ANY, ANY, ANY),
        scratch_shapes=[
            pltpu.VMEM((2 * half + 16 + NB, feat), F32),
            pltpu.SemaphoreType.DMA((6,)),
        ],
        name="prepare",
    )(where, feats, ridge)


def join_kernel(where_ref, own1, f1, g1, h1, piece, got, out, sems):
    full = own1.shape[0]
    row_idx, col_idx = where_ref[0], where_ref[1]
    top, low = out.at[pl.ds(0, full)], out.at[pl.ds(full, piece.shape[0])]
    mine = row_idx % 2 == col_idx % 8 // 4
    holder = row_idx == col_idx // 4 % 8
    picks = [
        (row_idx == 0, own1, top, 0),
        (row_idx == 2, f1, top, 0),
        (row_idx == 6, g1, top, 0),
        (row_idx == 4, h1, top, 0),
        (holder, piece, low, 1),
        (mine & jnp.logical_not(holder), got, low, 1),
    ]
    for test, src, dst, i in picks:

        @pl.when(test)
        def _(src=src, dst=dst, i=i):
            pltpu.make_async_copy(src, dst, sems.at[i]).start()

    @pl.when(row_idx % 2 == 1)
    def _():
        top[...] = jnp.zeros(top.shape, F32)

    @pl.when(jnp.logical_not(mine))
    def _():
        low[...] = jnp.zeros(low.shape, F32)

    for test, src, dst, i in picks:

        @pl.when(test)
        def _(src=src, dst=dst, i=i):
            pltpu.make_async_copy(src, dst, sems.at[i]).wait()


def join(where, *parts):
    rows = parts[0].shape[0] + parts[4].shape[0]
    return pl.pallas_call(
        join_kernel,
        out_shape=shaped(rows, parts[0].shape[1]),
        in_specs=[SM] + [ANY] * 6,
        out_specs=VM,
        scratch_shapes=[pltpu.SemaphoreType.DMA((2,))],
        name="join",
    )(where, *parts)


def moved(block, hop):
    links = []
    for device in range(768):
        x, c, z, y = device // 192, device // 96 % 2, device % 96 // 8, device % 8
        to = hop(x, c, y, z)
        if to is not None:
            near = (z + (to[2] if len(to) > 2 else 0)) % 12
            links.append((device, (to[0] % 4 * 2 + to[1]) * 96 + near * 8 + y))
    return lax.ppermute(block, ("row", "col"), links)


ANY = pl.BlockSpec(memory_space=pl.ANY)


def along(start, stop):
    return lambda x, c, y, z: (stop, 0) if (x, c) == (start, 0) else None


def fanned(x, c, y, z):
    turn = (x - z) % 4
    if turn == 2 or c != y // 4:
        return None
    return {0: (x + 1, c, 0), 3: (x - 1, c, -1), 1: (x + 2, c, 1)}[turn]


def per_device(features, ridge):
    tiles, _, width, feat = features.shape
    row_idx = lax.axis_index("row")
    col_idx = lax.axis_index("col")
    turn = (row_idx // 2 - col_idx // 8) % 4
    near = (col_idx // 8 + jnp.where(turn == 1, 1, jnp.where(turn == 3, -1, 0))) % 12
    where = jnp.stack([row_idx, col_idx, near * 8 + col_idx % 8]).astype(jnp.int32)
    feats = features.reshape(tiles, width, feat)
    own0, own1, piece = prepare(where, feats, ridge)
    g0 = moved(own0, along(0, 3))
    f0 = moved(own0, along(0, 1))
    d0 = moved(own0, along(0, 2))
    f1 = moved(own1, along(0, 1))
    a0 = jnp.where(row_idx == 0, own0, F32(0.0)) + f0 + g0 + d0
    b0 = moved(a0, lambda x, c, y, z: (x, 1) if c == 0 else None)
    g1 = moved(own1, along(0, 3))
    got = moved(piece, fanned)
    h1 = moved(f1, along(1, 2))
    rows = pltpu.with_memory_space_constraint(
        feats.reshape(tiles * width, feat), pltpu.HBM
    )
    kept = first_step(where, rows, (a0, b0))
    a1 = join(where, own1, f1, g1, h1, piece, got)
    b1 = moved(a1, lambda x, c, y, z: (x, 1 - c))
    schur, panel = second_step(where, rows, (a1, b1), ridge, kept)
    return (
        schur.reshape(tiles, 1, width, 1, 1, NB),
        panel.reshape(tiles, 1, width, width),
    )


def solution(mesh):
    in_specs = (P(None, "row", None, None), P(None, "row", None))
    out_specs = (P(None, "row", None, None, "col", None), P(None, "row", None, None))
    return jax.shard_map(
        per_device, mesh=mesh, in_specs=in_specs, out_specs=out_specs, check_vma=False
    )
```

```python
import jax
import jax.numpy as jnp
from jax import lax
from jax.experimental import pallas as pl
from jax.experimental.pallas import tpu as pltpu
from jax.sharding import PartitionSpec as P

F32 = jnp.float32
BF16 = jnp.bfloat16
NB = 128
TN = (((1,), (1,)), ((), ()))


def split(a):
    hi = a.astype(BF16)
    return hi, (a - hi.astype(F32)).astype(BF16)


def dot3(a, b):
    one = lambda x, y: lax.dot_general(x, y, TN, preferred_element_type=F32)
    return one(a[0], b[0]) + (one(a[0], b[1]) + one(a[1], b[0]))


def dotf(a, b):
    return lax.dot_general(
        a, b, TN, precision=lax.Precision.HIGHEST, preferred_element_type=F32
    )


def lanes(v, k):
    return jnp.broadcast_to(v[:, k : k + 1], (8, NB))


def micro(upper, inv, t, cols_ref):
    row, low, o = upper[t], inv[t], 8 * t
    for k in range(8):
        cols_ref[8 * k : 8 * k + 8, :] = lanes(row, o + k)
    s = {}
    for k in range(8):
        for i in range(k, 8):
            s[i, k] = jnp.broadcast_to(cols_ref[8 * k + i : 8 * k + i + 1, :], (8, NB))
    v = [jnp.broadcast_to(row[i : i + 1, :], (8, NB)) for i in range(8)]
    w = [jnp.broadcast_to(low[i : i + 1, :], (8, NB)) for i in range(8)]
    u = {r: [lanes(upper[r], o + k) for k in range(8)] for r in range(t + 1, 16)}
    scale = []
    for k in range(8):
        rs = lax.rsqrt(s[k, k])
        scale.append(rs)
        v[k] = v[k] * rs
        w[k] = w[k] * rs
        for i in range(k + 1, 8):
            s[i, k] = s[i, k] * rs
        for j in range(k + 1, 8):
            for i in range(j, 8):
                s[i, j] = s[i, j] - s[i, k] * s[j, k]
        for i in range(k + 1, 8):
            v[i] = v[i] - s[i, k] * v[k]
            w[i] = w[i] - s[i, k] * w[k]
    upper, inv = list(upper), list(inv)
    if t < 15:
        r = t + 1
        for k in range(8):
            c = u[r][k]
            for m in range(k):
                c = c - u[r][m] * s[k, m]
            c = c * scale[k]
            u[r][k] = c
            upper[r] = upper[r] - c * v[k]
            inv[r] = inv[r] - c * w[k]
    if t < 14:
        vb, wb = list(v), list(w)
        for k in range(7, -1, -1):
            for m in range(k + 1, 8):
                vb[k] = vb[k] - s[m, k] * vb[m]
                wb[k] = wb[k] - s[m, k] * wb[m]
            vb[k] = vb[k] * scale[k]
            wb[k] = wb[k] * scale[k]
        for r in range(t + 2, 16):
            for k in range(8):
                upper[r] = upper[r] - u[r][k] * vb[k]
                inv[r] = inv[r] - u[r][k] * wb[k]
    sub = lax.broadcasted_iota(jnp.int32, (8, NB), 0)
    a, b = v[0], w[0]
    for k in range(1, 8):
        a = jnp.where(sub == k, v[k], a)
        b = jnp.where(sub == k, w[k], b)
    upper[t], inv[t] = a, b
    return upper, inv


def factor(block, cols_ref, work=()):
    upper = [block[8 * i : 8 * i + 8, :] for i in range(16)]
    sub = lax.broadcasted_iota(jnp.int32, (8, NB), 0)
    lane = lax.broadcasted_iota(jnp.int32, (8, NB), 1)
    inv = [jnp.where(lane == sub + 8 * i, F32(1.0), F32(0.0)) for i in range(16)]
    for t in range(16):
        for job in work[len(work) * t // 16 : len(work) * (t + 1) // 16]:
            job()
        upper, inv = micro(upper, inv, t, cols_ref.at[64 * (t % 2) : 64 * (t % 2) + 64])
    return upper, inv


def tile_of(inner, width):
    return jnp.square(inner / width + 1.0)


def match(shape, delta):
    rows = lax.broadcasted_iota(jnp.int32, shape, 0)
    cols = lax.broadcasted_iota(jnp.int32, shape, 1)
    return rows - cols == delta


def kernel_tile(left, right, delta, ridge, feat):
    block = tile_of(dot3(left, right), feat)
    return block + jnp.where(match(block.shape, delta), ridge, F32(0.0))


STEP = 192
FAR = 1 << 20


def first_kernel(
    where_ref, rows_hbm, aa_ref, ab_ref, ba_ref, bb_ref,
    panel_hbm, p_hi, p_lo, pan_hi_hbm, pan_lo_hbm, line_ref, inv_hi, inv_lo, low_hi, low_lo,
    rows, kp, out, pan_hi, pan_lo, cols_ref, in_sem, out_sems,
):
    count, feat = rows.shape
    half = kp.shape[1]
    load = pltpu.make_async_copy(rows_hbm, rows, in_sem)
    load.start()
    row_idx = where_ref[0]
    pan_hi[:NB, :], pan_lo[:NB, :] = split(aa_ref[...] + ba_ref[...])
    pan_hi[NB:, :], pan_lo[NB:, :] = split(ab_ref[:NB, :] + bb_ref[:NB, :])
    line = ab_ref[NB : NB + 1, :half] + bb_ref[NB : NB + 1, :half]
    line_ref[...] = jnp.broadcast_to(line, (8, half))
    stores = [
        pltpu.make_async_copy(pan_hi, pan_hi_hbm, out_sems.at[0]),
        pltpu.make_async_copy(pan_lo, pan_lo_hbm, out_sems.at[1]),
        pltpu.make_async_copy(out.at[0], panel_hbm.at[:, pl.ds(0, NB)], out_sems.at[2]),
        pltpu.make_async_copy(out.at[1], panel_hbm.at[:, pl.ds(NB, NB)], out_sems.at[3]),
    ]
    stores[0].start()
    stores[1].start()
    pan = (pan_hi[...], pan_lo[...])
    k11 = kernel_tile(pan, (pan_hi[:NB, :], pan_lo[:NB, :]), 0, line[:, :NB], feat)
    k22 = kernel_tile(
        (pan_hi[NB:, :], pan_lo[NB:, :]), (pan_hi[NB:, :], pan_lo[NB:, :]), 0, line[:, NB:], feat
    )
    load.wait()

    def tiles(i):
        n = i * STEP
        x = split(rows[n : n + STEP, :])
        g = tile_of(dot3(x, (pan_hi[...], pan_lo[...])), feat)
        if n < 512:
            g = g + jnp.where(match(g.shape, jnp.where(row_idx == 0, -n, FAR)), line, F32(0.0))
        kp[n : n + STEP, :] = g

    _, inv = factor(k11[:NB], cols_ref, [lambda i=i: tiles(i) for i in range(count // STEP)])
    inv0 = jnp.concatenate(inv, axis=0)
    inv_hi[0], inv_lo[0] = split(inv0)
    l10 = dotf(k11[NB:], inv0)
    low_hi[...], low_lo[...] = split(l10)
    s11 = k22 - dotf(l10, l10)

    def solve(i):
        n = i * STEP
        x = dot3(split(kp[n : n + STEP, :NB]), (inv_hi[0], inv_lo[0]))
        out[0, n : n + STEP, :] = x
        hi, lo = split(x)
        p_hi[n : n + STEP, :NB], p_lo[n : n + STEP, :NB] = hi, lo
        kp[n : n + STEP, NB:] = kp[n : n + STEP, NB:] - dot3((hi, lo), (low_hi[...], low_lo[...]))

    _, inv = factor(s11, cols_ref, [lambda i=i: solve(i) for i in range(count // STEP)])
    stores[2].start()
    inv_hi[1], inv_lo[1] = split(jnp.concatenate(inv, axis=0))
    x = dot3(split(kp[:, NB:]), (inv_hi[1], inv_lo[1]))
    out[1] = x
    stores[3].start()
    p_hi[:, NB:], p_lo[:, NB:] = split(x)
    for store in stores:
        store.wait()


def second_kernel(
    where_ref, rows_hbm, a_ref, b_ref, h_ref, piece_ref, got_ref, ridge_ref, old_panel,
    p_hi, p_lo, pan_hi_hbm, pan_lo_hbm, line_ref, inv_hi, inv_lo, low_hi, low_lo,
    schur_ref, panel_hbm,
    rows, kp, out, q_hi, q_lo, l2_hi, l2_lo, l32_hi, l32_lo, nv_hi, nv_lo, col_hi, col_lo, kc, pc_hi, pc_lo,
    pan_hi, pan_lo, cols_ref, in_sems, out_sems,
):
    count, feat = rows.shape
    half = kp.shape[1]
    early = [
        pltpu.make_async_copy(pan_hi_hbm, pan_hi, in_sems.at[0]),
        pltpu.make_async_copy(pan_lo_hbm, pan_lo, in_sems.at[1]),
    ]
    load = pltpu.make_async_copy(rows_hbm, rows, in_sems.at[2])
    for copy in early + [load]:
        copy.start()
    row_idx, col_idx = where_ref[0], where_ref[1]
    q_hi[...], q_lo[...] = split(a_ref[:half, :] + b_ref[:half, :] + h_ref[:half, :])
    end = half + 1
    line = a_ref[half:end, :half] + b_ref[half:end, :half] + h_ref[half:end, :half]
    holder = row_idx == col_idx // 4 % 8
    col_hi[...], col_lo[...] = split(jnp.where(holder, piece_ref[...], got_ref[...]))
    new = (q_hi[...], q_lo[...])

    def lead(k, dst_hi, dst_lo):
        n0 = dot3(split(k[:, :NB]), (inv_hi[0], inv_lo[0]))
        s0 = split(n0)
        n1 = dot3(split(k[:, NB:] - dot3(s0, (low_hi[...], low_lo[...]))), (inv_hi[1], inv_lo[1]))
        s1 = split(n1)
        dst_hi[:, :NB], dst_lo[:, :NB] = s0
        dst_hi[:, NB:half], dst_lo[:, NB:half] = s1

    k2 = kernel_tile(new, new, 0, line, feat)
    for copy in early:
        copy.wait()
    lead(tile_of(dot3(new, (pan_hi[...], pan_lo[...])), feat), l2_hi, l2_lo)
    k2 = k2 - dot3((l2_hi[...], l2_lo[...]), (l2_hi[...], l2_lo[...]))
    load.wait()

    def tiles(i):
        n = i * STEP
        x = split(rows[n : n + STEP, :])
        g = tile_of(dot3(x, (q_hi[...], q_lo[...])), feat)
        if half - n > -STEP and n < 512:
            g = g + jnp.where(match(g.shape, jnp.where(row_idx == 0, half - n, FAR)), line, F32(0.0))
        kp[n : n + STEP, :] = g - dot3(
            (p_hi[n : n + STEP, :], p_lo[n : n + STEP, :]), (l2_hi[...], l2_lo[...])
        )

    _, inv = factor(k2[:NB, :NB], cols_ref, [lambda i=i: tiles(i) for i in range(count // STEP)])
    inv2 = jnp.concatenate(inv, axis=0)
    nv_hi[0], nv_lo[0] = split(inv2)
    l32 = dotf(k2[NB:, :NB], inv2)
    l32_hi[...], l32_lo[...] = split(l32)
    s33 = k2[NB:, NB:] - dotf(l32, l32)
    first = col_idx * NB
    owner, n_tile = (col_idx // 4) % 8, col_idx // 32
    inner = (col_idx % 4) * NB
    diag = ridge_ref[n_tile, :, pl.ds(pl.multiple_of(inner, NB), NB)]
    corner = jnp.where(row_idx == owner, n_tile * 512 + inner, FAR)

    def columns():
        col = (col_hi[...], col_lo[...])
        lead(
            kernel_tile(col, (pan_hi[...], pan_lo[...]), -first, line_ref[:1, :], feat),
            pc_hi, pc_lo,
        )
        kc[...] = kernel_tile(col, new, half - first, line, feat) - dot3(
            (pc_hi[:, :half], pc_lo[:, :half]), (l2_hi[...], l2_lo[...])
        )
        x = split(dot3(split(kc[:, :NB]), (nv_hi[0], nv_lo[0])))
        pc_hi[:, half : half + NB], pc_lo[:, half : half + NB] = x
        kc[:, NB:] = kc[:, NB:] - dot3(x, (l32_hi[...], l32_lo[...]))

    def solve(i):
        n = i * STEP
        x = dot3(split(kp[n : n + STEP, :NB]), (nv_hi[0], nv_lo[0]))
        out[0, n : n + STEP, :] = x
        s = split(x)
        kp[n : n + STEP, NB:] = kp[n : n + STEP, NB:] - dot3(s, (l32_hi[...], l32_lo[...]))
        g = tile_of(dot3(split(rows[n : n + STEP, :]), (col_hi[...], col_lo[...])), feat)
        g = g + jnp.where(match(g.shape, corner - n), diag, F32(0.0))
        g = g - dot3(
            (p_hi[n : n + STEP, :], p_lo[n : n + STEP, :]), (pc_hi[:, :half], pc_lo[:, :half])
        )
        schur_ref[n : n + STEP, :] = g - dot3(
            s, (pc_hi[:, half : half + NB], pc_lo[:, half : half + NB])
        )

    _, inv = factor(
        s33, cols_ref, [columns] + [lambda i=i: solve(i) for i in range(count // STEP)]
    )
    stores = [
        pltpu.make_async_copy(
            out.at[i], panel_hbm.at[:, pl.ds(half + i * NB, NB)], out_sems.at[i]
        )
        for i in range(2)
    ]
    stores[0].start()
    nv_hi[1], nv_lo[1] = split(jnp.concatenate(inv, axis=0))
    pc = split(dot3(split(kc[:, NB:]), (nv_hi[1], nv_lo[1])))
    x = dot3(split(kp[:, NB:]), (nv_hi[1], nv_lo[1]))
    out[1] = x
    stores[1].start()
    schur_ref[...] = schur_ref[...] - dot3(split(x), pc)
    for store in stores:
        store.wait()


VM = pl.BlockSpec(memory_space=pltpu.VMEM)
SM = pl.BlockSpec(memory_space=pltpu.SMEM)
HB = pl.BlockSpec(memory_space=pltpu.HBM)


def shaped(*shape, kind=F32):
    return jax.ShapeDtypeStruct(shape, kind)


def first_step(where, rows, parts):
    count, feat = rows.shape
    half = 256
    return pl.pallas_call(
        first_kernel,
        out_shape=(
            shaped(count, 2 * half),
            shaped(count, half, kind=BF16),
            shaped(count, half, kind=BF16),
            shaped(half, feat, kind=BF16),
            shaped(half, feat, kind=BF16),
            shaped(8, half),
            shaped(2, NB, NB, kind=BF16),
            shaped(2, NB, NB, kind=BF16),
            shaped(NB, NB, kind=BF16),
            shaped(NB, NB, kind=BF16),
        ),
        in_specs=[SM, HB] + [VM] * 4,
        out_specs=(HB, VM, VM, HB, HB) + (VM,) * 5,
        scratch_shapes=[
            pltpu.VMEM((count, feat), F32),
            pltpu.VMEM((count, half), F32),
            pltpu.VMEM((2, count, NB), F32),
            pltpu.VMEM((half, feat), BF16),
            pltpu.VMEM((half, feat), BF16),
            pltpu.VMEM((NB, NB), F32),
            pltpu.SemaphoreType.DMA,
            pltpu.SemaphoreType.DMA((4,)),
        ],
        compiler_params=pltpu.CompilerParams(vmem_limit_bytes=20 << 20),
        cost_estimate=pl.CostEstimate(flops=5 * 10**9, bytes_accessed=40 * 10**6, transcendentals=0),
        name="first_step",
    )(where, rows, *parts)


def second_step(where, rows, parts, ridge, kept):
    count, feat = rows.shape
    half = 256
    return pl.pallas_call(
        second_kernel,
        out_shape=(shaped(count, NB), shaped(count, 2 * half)),
        in_specs=[SM, HB] + [VM] * 6 + [HB, VM, VM, HB, HB] + [VM] * 5,
        out_specs=(VM, HB),
        input_output_aliases={8: 1},
        scratch_shapes=[
            pltpu.VMEM((count, feat), F32),
            pltpu.VMEM((count, half), F32),
            pltpu.VMEM((2, count, NB), F32),
            pltpu.VMEM((half, feat), BF16),
            pltpu.VMEM((half, feat), BF16),
            pltpu.VMEM((half, half), BF16),
            pltpu.VMEM((half, half), BF16),
            pltpu.VMEM((NB, NB), BF16),
            pltpu.VMEM((NB, NB), BF16),
            pltpu.VMEM((2, NB, NB), BF16),
            pltpu.VMEM((2, NB, NB), BF16),
            pltpu.VMEM((NB, feat), BF16),
            pltpu.VMEM((NB, feat), BF16),
            pltpu.VMEM((NB, half), F32),
            pltpu.VMEM((NB, half + NB), BF16),
            pltpu.VMEM((NB, half + NB), BF16),
            pltpu.VMEM((half, feat), BF16),
            pltpu.VMEM((half, feat), BF16),
            pltpu.VMEM((NB, NB), F32),
            pltpu.SemaphoreType.DMA((3,)),
            pltpu.SemaphoreType.DMA((2,)),
        ],
        compiler_params=pltpu.CompilerParams(vmem_limit_bytes=20 << 20),
        cost_estimate=pl.CostEstimate(flops=5 * 10**9, bytes_accessed=40 * 10**6, transcendentals=0),
        name="second_step",
    )(where, rows, *parts, ridge, *kept)


def prepare_kernel(where_ref, feats_ref, ridge_ref, own0a, own0b, own1, piece, buf, sems):
    half = own1.shape[0] - 8
    full = half + 8
    starts = (0, full, 2 * full)
    loads = [
        pltpu.make_async_copy(feats_ref.at[0, pl.ds(0, NB)], buf.at[pl.ds(0, NB)], sems.at[0]),
        pltpu.make_async_copy(feats_ref.at[0, pl.ds(NB, NB)], buf.at[pl.ds(NB, NB)], sems.at[3]),
        pltpu.make_async_copy(
            feats_ref.at[0, pl.ds(half, half)], buf.at[pl.ds(full, half)], sems.at[1]
        ),
        pltpu.make_async_copy(
            feats_ref.at[where_ref[2] // 32, pl.ds(pl.multiple_of(where_ref[2] % 4 * NB, NB), NB)],
            buf.at[pl.ds(2 * full, NB)],
            sems.at[2],
        ),
    ]
    stores = [
        pltpu.make_async_copy(buf.at[pl.ds(s, ref.shape[0])], ref, sems.at[4 + i])
        for i, (s, ref) in enumerate(zip((0, NB) + starts[1:], (own0a, own0b, own1, piece)))
    ]
    for load in loads:
        load.start()
    for h in range(2):
        low = starts[h] + half
        line = ridge_ref[0, :, h * half : (h + 1) * half]
        buf[low : low + 8, :half] = jnp.broadcast_to(line, (8, half))
        buf[low : low + 8, half:] = jnp.zeros((8, buf.shape[1] - half), F32)
    for load, store in zip(loads, stores):
        load.wait()
        store.start()
    for store in stores:
        store.wait()


def prepare(where, feats, ridge):
    half, feat = 256, feats.shape[2]
    return pl.pallas_call(
        prepare_kernel,
        out_shape=(shaped(NB, feat), shaped(NB + 8, feat), shaped(half + 8, feat), shaped(NB, feat)),
        in_specs=[SM, HB, VM],
        out_specs=(ANY, ANY, ANY, ANY),
        scratch_shapes=[
            pltpu.VMEM((2 * half + 16 + NB, feat), F32),
            pltpu.SemaphoreType.DMA((8,)),
        ],
        name="prepare",
    )(where, feats, ridge)


def moved(block, hop):
    links = []
    for device in range(768):
        x, c, z, y = device // 192, device // 96 % 2, device % 96 // 8, device % 8
        to = hop(x, c, y, z)
        if to is not None:
            near = (z + (to[2] if len(to) > 2 else 0)) % 12
            flat = to[3] if len(to) > 3 else y
            links.append((device, (to[0] % 4 * 2 + to[1]) * 96 + near * 8 + flat))
    return lax.ppermute(block, ("row", "col"), links)


ANY = pl.BlockSpec(memory_space=pl.ANY)


def along(start, stop):
    return lambda x, c, y, z: (stop, 0) if (x, c) == (start, 0) else None


def fanned(x, c, y, z):
    turn = (x - z) % 4
    same = y // 4 == c
    if turn == 2 and same:
        return None
    step, lift = {0: (1, 0), 3: (-1, -1), 1: (2, 1), 2: (0, 2)}[turn]
    return (x + step, c if same else 1 - c, lift, y if same else 7 - y)


def per_device(features, ridge):
    tiles, _, width, feat = features.shape
    row_idx = lax.axis_index("row")
    col_idx = lax.axis_index("col")
    y, z = col_idx % 8, col_idx // 8
    turn = (row_idx // 2 - z) % 4
    lift = jnp.where(turn == 1, 1, jnp.where(turn == 3, -1, jnp.where(turn == 2, 2, 0)))
    flat = jnp.where(y // 4 == row_idx % 2, y, 7 - y)
    where = jnp.stack([row_idx, col_idx, (z + lift) % 12 * 8 + flat]).astype(jnp.int32)
    feats = features.reshape(tiles, width, feat)
    own0a, own0b, own1, piece = prepare(where, feats, ridge)
    lead = row_idx == 0
    zero = F32(0.0)
    down = lambda x, c, y, z: (x, 1) if c == 0 else None
    f0a = moved(own0a, along(0, 1))
    g0b = moved(own0b, along(0, 3))
    f0b = moved(own0b, along(0, 1))
    g0a = moved(own0a, along(0, 3))
    f1 = moved(own1, along(0, 1))
    g1 = moved(own1, along(0, 3))
    ha = moved(f0a, along(1, 2))
    hb = moved(g0b, along(3, 2))
    a0a = jnp.where(lead, own0a, zero) + f0a + g0a + ha
    a0b = jnp.where(lead, own0b, zero) + f0b + g0b + hb
    b0a = moved(a0a, down)
    b0b = moved(a0b, down)
    a1 = jnp.where(lead, own1, zero) + f1 + g1
    b1 = moved(a1, lambda x, c, y, z: (x, 1) if c == 0 and x != 2 else None)
    h1 = moved(a1, lambda x, c, y, z: (2, x // 2) if c == 0 and x % 2 else None)
    got = moved(piece, fanned)
    rows = pltpu.with_memory_space_constraint(
        feats.reshape(tiles * width, feat), pltpu.HBM
    )
    kept = first_step(where, rows, (a0a, a0b, b0a, b0b))
    schur, panel = second_step(where, rows, (a1, b1, h1, piece, got), ridge, kept)
    return (
        schur.reshape(tiles, 1, width, 1, 1, NB),
        panel.reshape(tiles, 1, width, width),
    )


def solution(mesh):
    in_specs = (P(None, "row", None, None), P(None, "row", None))
    out_specs = (P(None, "row", None, None, "col", None), P(None, "row", None, None))
    return jax.shard_map(
        per_device, mesh=mesh, in_specs=in_specs, out_specs=out_specs, check_vma=False
    )
```

```python
import jax
import jax.numpy as jnp
from jax import lax
from jax.experimental import pallas as pl
from jax.experimental.pallas import tpu as pltpu
from jax.sharding import PartitionSpec as P

F32 = jnp.float32
BF16 = jnp.bfloat16
NB = 128
TN = (((1,), (1,)), ((), ()))


def split(a):
    hi = a.astype(BF16)
    return hi, (a - hi.astype(F32)).astype(BF16)


def dot3(a, b):
    one = lambda x, y: lax.dot_general(x, y, TN, preferred_element_type=F32)
    return one(a[0], b[0]) + (one(a[0], b[1]) + one(a[1], b[0]))


def dotf(a, b):
    return lax.dot_general(
        a, b, TN, precision=lax.Precision.HIGHEST, preferred_element_type=F32
    )


def lanes(v, k):
    return jnp.broadcast_to(v[:, k : k + 1], (8, NB))


def micro(upper, inv, t, cols_ref):
    row, low, o = upper[t], inv[t], 8 * t
    for k in range(8):
        cols_ref[8 * k : 8 * k + 8, :] = lanes(row, o + k)
    s = {}
    for k in range(8):
        for i in range(k, 8):
            s[i, k] = jnp.broadcast_to(cols_ref[8 * k + i : 8 * k + i + 1, :], (8, NB))
    v = [jnp.broadcast_to(row[i : i + 1, :], (8, NB)) for i in range(8)]
    w = [jnp.broadcast_to(low[i : i + 1, :], (8, NB)) for i in range(8)]
    u = {r: [lanes(upper[r], o + k) for k in range(8)] for r in range(t + 1, 16)}
    scale = []
    for k in range(8):
        rs = lax.rsqrt(s[k, k])
        scale.append(rs)
        v[k] = v[k] * rs
        w[k] = w[k] * rs
        for i in range(k + 1, 8):
            s[i, k] = s[i, k] * rs
        for j in range(k + 1, 8):
            for i in range(j, 8):
                s[i, j] = s[i, j] - s[i, k] * s[j, k]
        for i in range(k + 1, 8):
            v[i] = v[i] - s[i, k] * v[k]
            w[i] = w[i] - s[i, k] * w[k]
    upper, inv = list(upper), list(inv)
    if t < 15:
        r = t + 1
        for k in range(8):
            c = u[r][k]
            for m in range(k):
                c = c - u[r][m] * s[k, m]
            c = c * scale[k]
            u[r][k] = c
            upper[r] = upper[r] - c * v[k]
            inv[r] = inv[r] - c * w[k]
    if t < 14:
        vb, wb = list(v), list(w)
        for k in range(7, -1, -1):
            for m in range(k + 1, 8):
                vb[k] = vb[k] - s[m, k] * vb[m]
                wb[k] = wb[k] - s[m, k] * wb[m]
            vb[k] = vb[k] * scale[k]
            wb[k] = wb[k] * scale[k]
        for r in range(t + 2, 16):
            for k in range(8):
                upper[r] = upper[r] - u[r][k] * vb[k]
                inv[r] = inv[r] - u[r][k] * wb[k]
    sub = lax.broadcasted_iota(jnp.int32, (8, NB), 0)
    a, b = v[0], w[0]
    for k in range(1, 8):
        a = jnp.where(sub == k, v[k], a)
        b = jnp.where(sub == k, w[k], b)
    upper[t], inv[t] = a, b
    return upper, inv


def factor(block, cols_ref, work=()):
    upper = [block[8 * i : 8 * i + 8, :] for i in range(16)]
    sub = lax.broadcasted_iota(jnp.int32, (8, NB), 0)
    lane = lax.broadcasted_iota(jnp.int32, (8, NB), 1)
    inv = [jnp.where(lane == sub + 8 * i, F32(1.0), F32(0.0)) for i in range(16)]
    for t in range(16):
        for job in work[len(work) * t // 16 : len(work) * (t + 1) // 16]:
            job()
        upper, inv = micro(upper, inv, t, cols_ref.at[64 * (t % 2) : 64 * (t % 2) + 64])
    return upper, inv


def tile_of(inner, width):
    return jnp.square(inner / width + 1.0)


def match(shape, delta):
    rows = lax.broadcasted_iota(jnp.int32, shape, 0)
    cols = lax.broadcasted_iota(jnp.int32, shape, 1)
    return rows - cols == delta


def kernel_tile(left, right, delta, ridge, feat):
    block = tile_of(dot3(left, right), feat)
    return block + jnp.where(match(block.shape, delta), ridge, F32(0.0))


STEP = 192
FAR = 1 << 20


def first_kernel(
    where_ref, rows_hbm, aa_ref, ab_ref, ba_ref, bb_ref,
    panel_hbm, p_hi, p_lo, pan_hi_hbm, pan_lo_hbm, line_ref, inv_hi, inv_lo, low_hi, low_lo,
    rows, kp, out, pan_hi, pan_lo, cols_ref, in_sem, out_sems,
):
    count, feat = rows.shape
    half = kp.shape[1]
    load = pltpu.make_async_copy(rows_hbm, rows, in_sem)
    load.start()
    row_idx = where_ref[0]
    pan_hi[:NB, :], pan_lo[:NB, :] = split(aa_ref[...] + ba_ref[...])
    pan_hi[NB:, :], pan_lo[NB:, :] = split(ab_ref[:NB, :] + bb_ref[:NB, :])
    line = ab_ref[NB : NB + 1, :half] + bb_ref[NB : NB + 1, :half]
    line_ref[...] = jnp.broadcast_to(line, (8, half))
    stores = [
        pltpu.make_async_copy(pan_hi, pan_hi_hbm, out_sems.at[0]),
        pltpu.make_async_copy(pan_lo, pan_lo_hbm, out_sems.at[1]),
        pltpu.make_async_copy(out.at[0], panel_hbm.at[:, pl.ds(0, NB)], out_sems.at[2]),
        pltpu.make_async_copy(out.at[1], panel_hbm.at[:, pl.ds(NB, NB)], out_sems.at[3]),
    ]
    stores[0].start()
    stores[1].start()
    pan = (pan_hi[...], pan_lo[...])
    k11 = kernel_tile(pan, (pan_hi[:NB, :], pan_lo[:NB, :]), 0, line[:, :NB], feat)
    k22 = kernel_tile(
        (pan_hi[NB:, :], pan_lo[NB:, :]), (pan_hi[NB:, :], pan_lo[NB:, :]), 0, line[:, NB:], feat
    )
    load.wait()

    def tiles(i):
        n = i * STEP
        x = split(rows[n : n + STEP, :])
        g = tile_of(dot3(x, (pan_hi[...], pan_lo[...])), feat)
        if n < 512:
            g = g + jnp.where(match(g.shape, jnp.where(row_idx == 0, -n, FAR)), line, F32(0.0))
        kp[n : n + STEP, :] = g

    _, inv = factor(k11[:NB], cols_ref, [lambda i=i: tiles(i) for i in range(count // STEP)])
    inv0 = jnp.concatenate(inv, axis=0)
    inv_hi[0], inv_lo[0] = split(inv0)
    l10 = dotf(k11[NB:], inv0)
    low_hi[...], low_lo[...] = split(l10)
    s11 = k22 - dotf(l10, l10)

    def solve(i):
        n = i * STEP
        x = dot3(split(kp[n : n + STEP, :NB]), (inv_hi[0], inv_lo[0]))
        out[0, n : n + STEP, :] = x
        hi, lo = split(x)
        p_hi[n : n + STEP, :NB], p_lo[n : n + STEP, :NB] = hi, lo
        kp[n : n + STEP, NB:] = kp[n : n + STEP, NB:] - dot3((hi, lo), (low_hi[...], low_lo[...]))

    _, inv = factor(s11, cols_ref, [lambda i=i: solve(i) for i in range(count // STEP)])
    stores[2].start()
    inv_hi[1], inv_lo[1] = split(jnp.concatenate(inv, axis=0))
    x = dot3(split(kp[:, NB:]), (inv_hi[1], inv_lo[1]))
    out[1] = x
    stores[3].start()
    p_hi[:, NB:], p_lo[:, NB:] = split(x)
    for store in stores:
        store.wait()


def second_kernel(
    where_ref, rows_hbm, a_ref, b_ref, h_ref, piece_ref, got_ref, ridge_ref, old_panel,
    p_hi, p_lo, pan_hi_hbm, pan_lo_hbm, line_ref, inv_hi, inv_lo, low_hi, low_lo,
    schur_ref, panel_hbm,
    rows, kp, out, q_hi, q_lo, l2_hi, l2_lo, l32_hi, l32_lo, nv_hi, nv_lo, col_hi, col_lo, kc, pc_hi, pc_lo,
    pan_hi, pan_lo, cols_ref, in_sems, out_sems,
):
    count, feat = rows.shape
    half = kp.shape[1]
    early = [
        pltpu.make_async_copy(pan_hi_hbm, pan_hi, in_sems.at[0]),
        pltpu.make_async_copy(pan_lo_hbm, pan_lo, in_sems.at[1]),
    ]
    load = pltpu.make_async_copy(rows_hbm, rows, in_sems.at[2])
    for copy in early + [load]:
        copy.start()
    row_idx, col_idx = where_ref[0], where_ref[1]
    q_hi[...], q_lo[...] = split(a_ref[:half, :] + b_ref[:half, :] + h_ref[:half, :])
    end = half + 1
    line = a_ref[half:end, :half] + b_ref[half:end, :half] + h_ref[half:end, :half]
    col_hi[...], col_lo[...] = split(piece_ref[...] + got_ref[...])
    new = (q_hi[...], q_lo[...])

    def lead(k, dst_hi, dst_lo):
        n0 = dot3(split(k[:, :NB]), (inv_hi[0], inv_lo[0]))
        s0 = split(n0)
        n1 = dot3(split(k[:, NB:] - dot3(s0, (low_hi[...], low_lo[...]))), (inv_hi[1], inv_lo[1]))
        s1 = split(n1)
        dst_hi[:, :NB], dst_lo[:, :NB] = s0
        dst_hi[:, NB:half], dst_lo[:, NB:half] = s1

    k2 = kernel_tile(new, new, 0, line, feat)
    for copy in early:
        copy.wait()
    lead(tile_of(dot3(new, (pan_hi[...], pan_lo[...])), feat), l2_hi, l2_lo)
    k2 = k2 - dot3((l2_hi[...], l2_lo[...]), (l2_hi[...], l2_lo[...]))
    load.wait()

    def tiles(i):
        n = i * STEP
        x = split(rows[n : n + STEP, :])
        g = tile_of(dot3(x, (q_hi[...], q_lo[...])), feat)
        if half - n > -STEP and n < 512:
            g = g + jnp.where(match(g.shape, jnp.where(row_idx == 0, half - n, FAR)), line, F32(0.0))
        kp[n : n + STEP, :] = g - dot3(
            (p_hi[n : n + STEP, :], p_lo[n : n + STEP, :]), (l2_hi[...], l2_lo[...])
        )

    _, inv = factor(k2[:NB, :NB], cols_ref, [lambda i=i: tiles(i) for i in range(count // STEP)])
    inv2 = jnp.concatenate(inv, axis=0)
    nv_hi[0], nv_lo[0] = split(inv2)
    l32 = dotf(k2[NB:, :NB], inv2)
    l32_hi[...], l32_lo[...] = split(l32)
    s33 = k2[NB:, NB:] - dotf(l32, l32)
    first = col_idx * NB
    owner, n_tile = (col_idx // 4) % 8, col_idx // 32
    inner = (col_idx % 4) * NB
    diag = ridge_ref[n_tile, :, pl.ds(pl.multiple_of(inner, NB), NB)]
    corner = jnp.where(row_idx == owner, n_tile * 512 + inner, FAR)

    def columns():
        col = (col_hi[...], col_lo[...])
        lead(
            kernel_tile(col, (pan_hi[...], pan_lo[...]), -first, line_ref[:1, :], feat),
            pc_hi, pc_lo,
        )
        kc[...] = kernel_tile(col, new, half - first, line, feat) - dot3(
            (pc_hi[:, :half], pc_lo[:, :half]), (l2_hi[...], l2_lo[...])
        )
        x = split(dot3(split(kc[:, :NB]), (nv_hi[0], nv_lo[0])))
        pc_hi[:, half : half + NB], pc_lo[:, half : half + NB] = x
        kc[:, NB:] = kc[:, NB:] - dot3(x, (l32_hi[...], l32_lo[...]))

    def solve(i):
        n = i * STEP
        x = dot3(split(kp[n : n + STEP, :NB]), (nv_hi[0], nv_lo[0]))
        out[0, n : n + STEP, :] = x
        s = split(x)
        kp[n : n + STEP, NB:] = kp[n : n + STEP, NB:] - dot3(s, (l32_hi[...], l32_lo[...]))
        g = tile_of(dot3(split(rows[n : n + STEP, :]), (col_hi[...], col_lo[...])), feat)
        g = g + jnp.where(match(g.shape, corner - n), diag, F32(0.0))
        g = g - dot3(
            (p_hi[n : n + STEP, :], p_lo[n : n + STEP, :]), (pc_hi[:, :half], pc_lo[:, :half])
        )
        schur_ref[n : n + STEP, :] = g - dot3(
            s, (pc_hi[:, half : half + NB], pc_lo[:, half : half + NB])
        )

    _, inv = factor(
        s33, cols_ref, [columns] + [lambda i=i: solve(i) for i in range(count // STEP)]
    )
    stores = [
        pltpu.make_async_copy(
            out.at[i], panel_hbm.at[:, pl.ds(half + i * NB, NB)], out_sems.at[i]
        )
        for i in range(2)
    ]
    stores[0].start()
    nv_hi[1], nv_lo[1] = split(jnp.concatenate(inv, axis=0))
    pc = split(dot3(split(kc[:, NB:]), (nv_hi[1], nv_lo[1])))
    x = dot3(split(kp[:, NB:]), (nv_hi[1], nv_lo[1]))
    out[1] = x
    stores[1].start()
    schur_ref[...] = schur_ref[...] - dot3(split(x), pc)
    for store in stores:
        store.wait()


VM = pl.BlockSpec(memory_space=pltpu.VMEM)
SM = pl.BlockSpec(memory_space=pltpu.SMEM)
HB = pl.BlockSpec(memory_space=pltpu.HBM)


def shaped(*shape, kind=F32):
    return jax.ShapeDtypeStruct(shape, kind)


def first_step(where, rows, parts):
    count, feat = rows.shape
    half = 256
    return pl.pallas_call(
        first_kernel,
        out_shape=(
            shaped(count, 2 * half),
            shaped(count, half, kind=BF16),
            shaped(count, half, kind=BF16),
            shaped(half, feat, kind=BF16),
            shaped(half, feat, kind=BF16),
            shaped(8, half),
            shaped(2, NB, NB, kind=BF16),
            shaped(2, NB, NB, kind=BF16),
            shaped(NB, NB, kind=BF16),
            shaped(NB, NB, kind=BF16),
        ),
        in_specs=[SM, HB] + [VM] * 4,
        out_specs=(HB, VM, VM, HB, HB) + (VM,) * 5,
        scratch_shapes=[
            pltpu.VMEM((count, feat), F32),
            pltpu.VMEM((count, half), F32),
            pltpu.VMEM((2, count, NB), F32),
            pltpu.VMEM((half, feat), BF16),
            pltpu.VMEM((half, feat), BF16),
            pltpu.VMEM((NB, NB), F32),
            pltpu.SemaphoreType.DMA,
            pltpu.SemaphoreType.DMA((4,)),
        ],
        compiler_params=pltpu.CompilerParams(vmem_limit_bytes=20 << 20),
        cost_estimate=pl.CostEstimate(flops=5 * 10**9, bytes_accessed=40 * 10**6, transcendentals=0),
        name="first_step",
    )(where, rows, *parts)


def second_step(where, rows, parts, ridge, kept):
    count, feat = rows.shape
    half = 256
    return pl.pallas_call(
        second_kernel,
        out_shape=(shaped(count, NB), shaped(count, 2 * half)),
        in_specs=[SM, HB] + [VM] * 6 + [HB, VM, VM, HB, HB] + [VM] * 5,
        out_specs=(VM, HB),
        input_output_aliases={8: 1},
        scratch_shapes=[
            pltpu.VMEM((count, feat), F32),
            pltpu.VMEM((count, half), F32),
            pltpu.VMEM((2, count, NB), F32),
            pltpu.VMEM((half, feat), BF16),
            pltpu.VMEM((half, feat), BF16),
            pltpu.VMEM((half, half), BF16),
            pltpu.VMEM((half, half), BF16),
            pltpu.VMEM((NB, NB), BF16),
            pltpu.VMEM((NB, NB), BF16),
            pltpu.VMEM((2, NB, NB), BF16),
            pltpu.VMEM((2, NB, NB), BF16),
            pltpu.VMEM((NB, feat), BF16),
            pltpu.VMEM((NB, feat), BF16),
            pltpu.VMEM((NB, half), F32),
            pltpu.VMEM((NB, half + NB), BF16),
            pltpu.VMEM((NB, half + NB), BF16),
            pltpu.VMEM((half, feat), BF16),
            pltpu.VMEM((half, feat), BF16),
            pltpu.VMEM((NB, NB), F32),
            pltpu.SemaphoreType.DMA((3,)),
            pltpu.SemaphoreType.DMA((2,)),
        ],
        compiler_params=pltpu.CompilerParams(vmem_limit_bytes=20 << 20),
        cost_estimate=pl.CostEstimate(flops=5 * 10**9, bytes_accessed=40 * 10**6, transcendentals=0),
        name="second_step",
    )(where, rows, *parts, ridge, *kept)


def prepare_kernel(where_ref, feats_ref, ridge_ref, own0a, own0b, own1, piece, buf, sems):
    half = own1.shape[0] - 8
    full = half + 8
    starts = (0, full, 2 * full)
    loads = [
        pltpu.make_async_copy(feats_ref.at[0, pl.ds(0, NB)], buf.at[pl.ds(0, NB)], sems.at[0]),
        pltpu.make_async_copy(feats_ref.at[0, pl.ds(NB, NB)], buf.at[pl.ds(NB, NB)], sems.at[3]),
        pltpu.make_async_copy(
            feats_ref.at[0, pl.ds(half, half)], buf.at[pl.ds(full, half)], sems.at[1]
        ),
        pltpu.make_async_copy(
            feats_ref.at[where_ref[2] // 32, pl.ds(pl.multiple_of(where_ref[2] % 4 * NB, NB), NB)],
            buf.at[pl.ds(2 * full, NB)],
            sems.at[2],
        ),
    ]
    stores = [
        pltpu.make_async_copy(buf.at[pl.ds(s, ref.shape[0])], ref, sems.at[4 + i])
        for i, (s, ref) in enumerate(zip((0, NB) + starts[1:], (own0a, own0b, own1, piece)))
    ]
    for load in loads:
        load.start()
    for h in range(2):
        low = starts[h] + half
        line = ridge_ref[0, :, h * half : (h + 1) * half]
        buf[low : low + 8, :half] = jnp.broadcast_to(line, (8, half))
        buf[low : low + 8, half:] = jnp.zeros((8, buf.shape[1] - half), F32)
    for load, store in zip(loads, stores):
        load.wait()
        store.start()
    for store in stores:
        store.wait()


def prepare(where, feats, ridge):
    half, feat = 256, feats.shape[2]
    return pl.pallas_call(
        prepare_kernel,
        out_shape=(shaped(NB, feat), shaped(NB + 8, feat), shaped(half + 8, feat), shaped(NB, feat)),
        in_specs=[SM, HB, VM],
        out_specs=(ANY, ANY, ANY, ANY),
        scratch_shapes=[
            pltpu.VMEM((2 * half + 16 + NB, feat), F32),
            pltpu.SemaphoreType.DMA((8,)),
        ],
        name="prepare",
    )(where, feats, ridge)


def moved(block, hop):
    links = []
    for device in range(768):
        x, c, z, y = device // 192, device // 96 % 2, device % 96 // 8, device % 8
        to = hop(x, c, y, z)
        if to is not None:
            near = (z + (to[2] if len(to) > 2 else 0)) % 12
            flat = to[3] if len(to) > 3 else y
            links.append((device, (to[0] % 4 * 2 + to[1]) * 96 + near * 8 + flat))
    return lax.ppermute(block, ("row", "col"), links)


ANY = pl.BlockSpec(memory_space=pl.ANY)


def along(start, stop):
    return lambda x, c, y, z: (stop, 0) if (x, c) == (start, 0) else None


def fanned(step):
    return lambda x, c, y, z: (x + step, c) if (x, c) == (z % 4, y // 4) else None


def per_device(features, ridge):
    tiles, _, width, feat = features.shape
    row_idx = lax.axis_index("row")
    col_idx = lax.axis_index("col")
    where = jnp.stack([row_idx, col_idx, col_idx]).astype(jnp.int32)
    feats = features.reshape(tiles, width, feat)
    own0a, own0b, own1, piece = prepare(where, feats, ridge)
    lead = row_idx == 0
    zero = F32(0.0)
    down = lambda x, c, y, z: (x, 1) if c == 0 else None
    f0a = moved(own0a, along(0, 1))
    g0b = moved(own0b, along(0, 3))
    f0b = moved(own0b, along(0, 1))
    g0a = moved(own0a, along(0, 3))
    f1 = moved(own1, along(0, 1))
    g1 = moved(own1, along(0, 3))
    ha = moved(f0a, along(1, 2))
    hb = moved(g0b, along(3, 2))
    a0a = jnp.where(lead, own0a, zero) + f0a + g0a + ha
    a0b = jnp.where(lead, own0b, zero) + f0b + g0b + hb
    b0a = moved(a0a, down)
    b0b = moved(a0b, down)
    a1 = jnp.where(lead, own1, zero) + f1 + g1
    b1 = moved(a1, lambda x, c, y, z: (x, 1) if c == 0 and x != 2 else None)
    h1 = moved(a1, lambda x, c, y, z: (2, x // 2) if c == 0 and x % 2 else None)
    c1 = moved(piece, fanned(1))
    c2 = moved(piece, fanned(3))
    c3 = moved(piece, fanned(2))
    rows = pltpu.with_memory_space_constraint(
        feats.reshape(tiles * width, feat), pltpu.HBM
    )
    kept = first_step(where, rows, (a0a, a0b, b0a, b0b))
    holder = row_idx == col_idx // 4 % 8
    ca = jnp.where(holder, piece, zero) + c1 + c2 + c3
    cb = moved(ca, lambda x, c, y, z: (x, 1 - c) if c == y // 4 else None)
    schur, panel = second_step(where, rows, (a1, b1, h1, ca, cb), ridge, kept)
    return (
        schur.reshape(tiles, 1, width, 1, 1, NB),
        panel.reshape(tiles, 1, width, width),
    )


def solution(mesh):
    in_specs = (P(None, "row", None, None), P(None, "row", None))
    out_specs = (P(None, "row", None, None, "col", None), P(None, "row", None, None))
    return jax.shard_map(
        per_device, mesh=mesh, in_specs=in_specs, out_specs=out_specs, check_vma=False
    )
```
